32 devices in a mesh: tm: 4 (over y, core), height: 4 (over z), width: 2 (over x).
Axes of the slice: x: 2, y: 2, z: 4, core: 2. Of those that a mesh axis runs over, the one named last changes fastest.
Arguments:
- tokens: bfloat16 [2048, 3072], P(('tm', 'height', 'width'))
- shift_mod: float32 [3072], replicated, may hold values from -3 to 3
- scale_mod: float32 [3072], replicated, may hold values from -2.5 to 2.5
- proj_weight: bfloat16 [64, 3072], replicated, may hold values from -0.109375 to 0.109375
- proj_bias: float32 [64], replicated, may hold values from -3 to 3
- conv1_weight: bfloat16 [3, 3, 3, 16, 512], replicated, may hold values from -0.3125 to 0.3125
- conv1_bias: float32 [512], replicated, may hold values from -3 to 3
- norm_gain: float32 [512], replicated, may hold values from 0.25 to 1.75
- norm_bias: float32 [512], replicated, may hold values from -3 to 3
- conv2_weight: bfloat16 [3, 3, 3, 512, 512], P(None, None, None, 'width'), may hold values from -0.0546875 to 0.0546875
- conv2_bias: float32 [512], replicated, may hold values from -3 to 3
Outputs:
- pixels: bfloat16 [16, 32, 16, 512], P('tm', 'height', 'width')
The draws below stay inside these ranges and needn't reach their ends.
All inputs are finite; a program needn't handle non-finite values.
Results may differ from the reference program's by a relative error of at most 0.0095.
Values may be sent and summed in bfloat16 or wider, within the bound.
No kernel may reach another device: no remote copies, remote signals or barrier semaphores. Data moves between devices by JAX's collectives and lax.ppermute only.
A program may use at most 128 MiB of HBM per device.

```python
import jax
import jax.numpy as jnp
from jax import lax

D = 3072
LAT = 16
C1 = 512
C2 = 512
GROUPS = 32
PF = 64
NT = 16
NH = 32
NW = 16
HP = 16
WP = 8
TOKENS = 2048


def draw_tokens(key, part):
    noise_key, dir_key = jax.random.split(jax.random.fold_in(key, 11))
    position = jnp.arange(TOKENS)
    frame_index = (position // (HP * WP)).astype(jnp.float32)
    direction = jax.random.normal(dir_key, (D,), jnp.float32)
    noise = jax.random.normal(noise_key, (TOKENS, D), jnp.float32)
    amplitude = 3.0 * frame_index / max(NT - 1, 1)
    return (noise + amplitude[:, None] * direction[None, :]).astype(jnp.bfloat16)


def level_of(key, extent, cuts, least, largest):
    factor_of, own = 1.0, jax.random.fold_in(key, 6)
    for dim, blocks in cuts:
        steps = jnp.exp(jax.random.uniform(jax.random.fold_in(own, dim), (blocks,), jnp.float32, least / len(cuts), largest / len(cuts)))
        factor_of = factor_of * jnp.repeat(steps, extent[dim] // blocks).reshape([-1 if axis == dim else 1 for axis in range(len(extent))])
    return factor_of


def normal_values(stream_key, shape, scale, limit, cuts=(), kind=jnp.bfloat16):
    level = level_of(stream_key, shape, cuts, -0.22, 0.18) if cuts else 1.0
    values = jax.random.normal(stream_key, shape, jnp.float32) * scale * level
    return jnp.minimum(jnp.maximum(values, -limit), limit).astype(kind)


def setup_inputs(seed: int = 0) -> dict:
    key_of = jax.random.split(jax.random.key(seed), 12)
    tokens = draw_tokens(jax.random.fold_in(key_of[11], 71), 0)
    shift_mod = normal_values(key_of[1], (D,), 0.5, 3.0, (), jnp.float32)
    scale_mod = normal_values(key_of[2], (D,), 0.3, 2.5, (), jnp.float32)
    proj_weight = normal_values(key_of[3], (PF, D), D ** -0.5, 0.109375)
    proj_bias = normal_values(key_of[4], (PF,), 0.5, 3.0, (), jnp.float32)
    conv1_weight = normal_values(key_of[5], (3, 3, 3, LAT, C1), (27 * LAT) ** -0.5, 0.3125)
    conv1_bias = normal_values(key_of[6], (C1,), 0.5, 3.0, (), jnp.float32)
    norm_gain = jnp.clip(1.0 + 0.15 * jax.random.normal(key_of[7], (C1,), jnp.float32), 0.25, 1.75)
    norm_bias = normal_values(key_of[8], (C1,), 0.5, 3.0, (), jnp.float32)
    conv2_weight = normal_values(key_of[9], (3, 3, 3, C1, C2), (27 * C1) ** -0.5, 0.0546875, ((3, 2),))
    conv2_bias = normal_values(key_of[10], (C2,), 0.5, 3.0, (), jnp.float32)
    return {"tokens": tokens, "shift_mod": shift_mod, "scale_mod": scale_mod, "proj_weight": proj_weight, "proj_bias": proj_bias, "conv1_weight": conv1_weight, "conv1_bias": conv1_bias, "norm_gain": norm_gain, "norm_bias": norm_bias, "conv2_weight": conv2_weight, "conv2_bias": conv2_bias}


def causal_conv(field, weight):
    result = lax.conv_general_dilated(field.astype(jnp.float32)[None], weight.astype(jnp.float32), (1, 1, 1), [(2, 0), (1, 1), (1, 1)], dimension_numbers=('NDHWC', 'DHWIO', 'NDHWC'), precision=lax.Precision.HIGHEST)
    return result[0]

def reference(tokens, shift_mod, scale_mod, proj_weight, proj_bias, conv1_weight, conv1_bias, norm_gain, norm_bias, conv2_weight, conv2_bias):
    values = tokens.astype(jnp.float32)
    center = lax.optimization_barrier(jnp.mean(values, axis=-1, keepdims=True))
    spread = lax.optimization_barrier(jnp.mean((values - center) * (values - center), axis=-1, keepdims=True))
    normed = ((values - center) * lax.rsqrt(spread + 1e-06) * (1.0 + scale_mod) + shift_mod).astype(jnp.bfloat16)
    projected = lax.dot_general(normed, proj_weight, (((1,), (1,)), ((), ())), preferred_element_type=jnp.float32)
    patches = (projected + proj_bias).astype(jnp.bfloat16)
    latent = patches.reshape(NT, HP, WP, LAT, 2, 2).transpose(0, 1, 4, 2, 5, 3).reshape(NT, NH, NW, LAT)
    hidden = (causal_conv(latent, conv1_weight) + conv1_bias).astype(jnp.bfloat16)
    grouped = hidden.astype(jnp.float32).reshape(NT, NH, NW, GROUPS, C1 // GROUPS)
    count = NT * NH * NW * (C1 // GROUPS)
    gmean = lax.optimization_barrier(jnp.sum(grouped, axis=(0, 1, 2, 4))) / count
    gvar = lax.optimization_barrier(jnp.sum(grouped * grouped, axis=(0, 1, 2, 4))) / count - gmean * gmean
    scaled = (grouped - gmean[:, None]) * lax.rsqrt(gvar + 1e-06)[:, None]
    scaled = scaled.reshape(NT, NH, NW, C1) * norm_gain + norm_bias
    activated = jax.nn.silu(scaled).astype(jnp.bfloat16)
    return (causal_conv(activated, conv2_weight) + conv2_bias).astype(jnp.bfloat16)
```

```python
import jax
import jax.numpy as jnp
from jax import lax
from jax.experimental import pallas as pl
from jax.experimental.pallas import tpu as pltpu
from jax.sharding import PartitionSpec as P

GROUPS = 32
FRAMES = 4
ROWS = 8
COLS = 8
AXES = ("tm", "height", "width")
bf16 = jnp.bfloat16
f32 = jnp.float32


def project_kernel(tok_ref, shift_ref, scale_ref, weight_ref, bias_ref, out_ref):
    values = tok_ref[...].astype(f32)
    center = jnp.mean(values, axis=-1, keepdims=True)
    values = values - center
    spread = jnp.mean(values * values, axis=-1, keepdims=True)
    normed = (values * lax.rsqrt(spread + 1e-06) * (1.0 + scale_ref[...]) + shift_ref[...]).astype(bf16)
    patches = lax.dot_general(normed, weight_ref[...], (((1,), (1,)), ((), ())), preferred_element_type=f32)
    patches = (patches + bias_ref[...]).astype(bf16)
    size = patches.shape[1]
    lat = size // 4
    source = lax.broadcasted_iota(jnp.int32, (size, size), 0)
    target = lax.broadcasted_iota(jnp.int32, (size, size), 1)
    wanted = 4 * (target % lat) + target // lat
    order = jnp.where(source == wanted, 1.0, 0.0).astype(bf16)
    patches = jnp.dot(patches, order, preferred_element_type=f32)
    half = patches.shape[0] // 2
    out_ref[...] = jnp.concatenate([patches[:half], patches[half:]], axis=1).astype(bf16)


def project(tokens, shift_mod, scale_mod, proj_weight, proj_bias):
    count, features = tokens.shape[0], proj_weight.shape[0]
    return pl.pallas_call(
        project_kernel,
        out_shape=jax.ShapeDtypeStruct((count // 2, 2 * features), bf16),
        name="project",
    )(tokens, shift_mod[None], scale_mod[None], proj_weight, proj_bias[None])


def decode_kernel(
    pos_ref,
    latent_ref,
    w1_ref,
    b1_ref,
    gain_ref,
    nbias_ref,
    w2_hbm,
    own_ref,
    other_ref,
    window,
    banded,
    hidden,
    field,
    cols,
    total,
    w2_ref,
    sem,
    *,
    NT,
    HP,
    WP,
    FT,
    TH,
    TW,
):
    C = w1_ref.shape[4]
    LAT = w1_ref.shape[3]
    C2 = w2_ref.shape[4]
    W = 2 * WP
    copy = pltpu.make_async_copy(w2_hbm, w2_ref, sem)
    copy.start()
    tm, height, width = pos_ref[0], pos_ref[1], pos_ref[2]

    for a in range(3):
        for v in range(2):
            for z in range(2):
                for i in range(2):
                    for j in range(2):
                        row = i if v == 0 else (-1 if i == 1 else 2)
                        col = j if z == 0 else (-1 if j == 1 else 2)
                        start = a * 16 * LAT + (((v * 2 + z) * 2 + i) * 2 + j) * LAT
                        for oi in range(2):
                            for oj in range(2):
                                b, e = row - oi + 1, col - oj + 1
                                at = (oi * 2 + oj) * C
                                if 0 <= b < 3 and 0 <= e < 3:
                                    banded[start : start + LAT, at : at + C] = w1_ref[a, b, e]
                                else:
                                    banded[start : start + LAT, at : at + C] = jnp.zeros((LAT, C), bf16)

    rows = latent_ref.shape[1]
    PR = rows // WP
    chunks = HP * WP // (2 * rows)
    frame_rows = HP * WP
    LN = 8 * LAT
    window[0 : 2 * frame_rows, :] = jnp.zeros((2 * frame_rows, 2 * LN), bf16)
    lane = lax.broadcasted_iota(jnp.int32, (rows, LN), 1)
    q = lax.broadcasted_iota(jnp.int32, (rows, LN), 0) % WP
    j_one = (lane // LAT) % 2 == 1
    low = lane < LN // 2
    keep = (j_one & (q > 0)) | (jnp.logical_not(j_one) & (q < WP - 1))
    i_one = (lax.broadcasted_iota(jnp.int32, (frame_rows, LN), 1) // (2 * LAT)) % 2 == 1

    def frame_body(t, carry):
        pieces = []
        for k in range(chunks):
            x = latent_ref[t * chunks + k].astype(f32)
            z = jnp.where(j_one, pltpu.roll(x, 1, 0), pltpu.roll(x, rows - 1, 0))
            z = jnp.where(keep, z, 0.0)
            zr = pltpu.roll(z, LN // 2, 1)
            xr = pltpu.roll(x, LN // 2, 1)
            pieces.append(jnp.where(low, x, zr))
            pieces.append(jnp.where(low, xr, z))
        y = jnp.concatenate(pieces, axis=0)
        zero = jnp.zeros((WP, LN), f32)
        above = jnp.concatenate([zero, y[:-WP]], axis=0)
        below = jnp.concatenate([y[WP:], zero], axis=0)
        v = jnp.where(i_one, above, below)
        base = pl.multiple_of((t + 2) * frame_rows, frame_rows)
        window[pl.ds(base, frame_rows), 0:LN] = y.astype(bf16)
        window[pl.ds(base, frame_rows), LN : 2 * LN] = v.astype(bf16)
        return carry

    lax.fori_loop(0, NT, frame_body, 0)

    FC = 4
    M = FC * frame_rows
    bias = b1_ref[...]
    sums = []
    squares = []
    hidden[:, 0:2, :, :, :] = jnp.zeros((4, 2, HP, WP, C), f32)
    for n in range(4):

        def chunk_body(g, carry, n=n):
            s, sq = carry
            at = pl.multiple_of(g * M, M)
            taps = jnp.concatenate(
                [window[pl.ds(pl.multiple_of(at + a * frame_rows, frame_rows), M), :] for a in range(3)], axis=1
            )
            h = jnp.dot(taps, banded[:, n * C : (n + 1) * C], preferred_element_type=f32) + bias
            hidden[n, pl.ds(g * FC + 2, FC)] = h.reshape(FC, HP, WP, C)
            h8 = h.reshape(M // 8, 8, C)
            return s + jnp.sum(h8, axis=0), sq + jnp.sum(h8 * h8, axis=0)

        s, sq = lax.fori_loop(0, NT // FC, chunk_body, (jnp.zeros((8, C), f32), jnp.zeros((8, C), f32)))
        sums.append(s)
        squares.append(sq)
    s = sums[0] + sums[1] + sums[2] + sums[3]
    sq = squares[0] + squares[1] + squares[2] + squares[3]
    s = jnp.broadcast_to(jnp.sum(s, axis=0, keepdims=True), (8, C))
    sq = jnp.broadcast_to(jnp.sum(sq, axis=0, keepdims=True), (8, C))
    size = gain_ref.shape[1] * lax.axis_size("width") // GROUPS
    member = jnp.where(
        lax.broadcasted_iota(jnp.int32, (C, C), 0) // size == lax.broadcasted_iota(jnp.int32, (C, C), 1) // size, 1.0, 0.0
    )
    count = NT * HP * WP * 4 * size
    gmean = jnp.dot(s, member, preferred_element_type=f32, precision=lax.Precision.HIGHEST)[0:1] / count
    second = jnp.dot(sq, member, preferred_element_type=f32, precision=lax.Precision.HIGHEST)[0:1] / count
    gvar = second - gmean * gmean
    inverse = lax.rsqrt(gvar + 1e-06)
    gain = gain_ref[...]
    nbias = nbias_ref[...]

    R = TH + 2
    PADW = W + 16
    edge = jnp.zeros(field.shape[:2] + (1, 128), f32)
    field[:, :, 7:8, :] = edge
    field[:, :, 8 + W : 9 + W, :] = edge
    first = height * (TH // 2) - 1

    def act_body(t, carry):
        frame = tm * FT + t
        for pp in range(TH // 2 + 2):
            prow = first + pp
            source = jnp.clip(prow, 0, HP - 1)
            inside = (frame >= 2) & (prow >= 0) & (prow < HP)
            for oi in range(2):
                row = 2 * pp + oi - 1
                if row < 0 or row >= R:
                    continue
                for oj in range(2):
                    h = hidden[oi * 2 + oj, frame, source].astype(bf16).astype(f32)
                    scaled = (h - gmean) * inverse * gain + nbias
                    act = scaled / (1.0 + jnp.exp(-scaled))
                    act = jnp.where(inside, act, 0.0)
                    for plane in range(field.shape[0]):
                        part = act[:, plane * 128 : (plane + 1) * 128]
                        if C < 128:
                            part = jnp.concatenate([part, jnp.zeros((WP, 128 - C), f32)], axis=1)
                        field[plane, t * R + row, pl.ds(8 + oj, WP, stride=2), :] = part
        return carry

    lax.fori_loop(0, FT + 2, act_body, 0)

    def cols_body(t, carry):
        for r in range(R):
            for e in range(3):
                for plane in range(field.shape[0]):
                    lanes = min(C, 128)
                    at = e * C + plane * 128
                    part = field[plane, t * R + r, 7 + e : 7 + e + W, :]
                    cols[t, r, :, at : at + lanes] = part[:, :lanes].astype(bf16)
        return carry

    lax.fori_loop(0, FT + 2, cols_body, 0)

    copy.wait()
    M2 = FT * TH * W
    for a in range(3):
        for b in range(3):
            taps = cols[a : a + FT, b : b + TH].reshape(M2, 3 * C)
            part = jnp.dot(taps, w2_ref[a, b].reshape(3 * C, C2), preferred_element_type=f32)
            if a == 0 and b == 0:
                total[...] = part
            else:
                total[...] += part

    tiles = W // TW
    result = total[...].reshape(FT * TH, tiles, TW, C2)
    if tiles == 2:
        mine = width == 0
        own_ref[...] = jnp.where(mine, result[:, 0], result[:, 1])
        other_ref[0] = jnp.where(mine, result[:, 1], result[:, 0]).astype(bf16)
    else:
        for k in range(tiles):

            @pl.when(width == k)
            def _(k=k):
                own_ref[...] = result[:, k]
                for step in range(1, tiles):
                    other_ref[step - 1] = result[:, (k + step) % tiles].astype(bf16)


def per_device(
    tokens,
    shift_mod,
    scale_mod,
    proj_weight,
    proj_bias,
    conv1_weight,
    conv1_bias,
    norm_gain,
    norm_bias,
    conv2_weight,
    conv2_bias,
    *,
    clip,
):
    width_count = lax.axis_size("width")
    height_count = lax.axis_size("height")
    time_count = lax.axis_size("tm")
    devices = width_count * height_count * time_count
    NT, NH, NW = clip
    FT, TH, TW = FRAMES, ROWS, COLS
    C2 = conv2_weight.shape[4]
    HP, WP = NH // 2, NW // 2
    C = conv2_weight.shape[3]
    LAT = conv1_weight.shape[3]

    chunk = project(tokens, shift_mod, scale_mod, proj_weight, proj_bias)
    spread = jnp.broadcast_to(chunk[None], (devices,) + chunk.shape)
    latent = lax.all_to_all(spread, AXES, 0, 0, tiled=True)

    width = lax.axis_index("width")
    position = jnp.stack([lax.axis_index("tm"), lax.axis_index("height"), width]).astype(jnp.int32)
    take = lambda x, axis: lax.dynamic_slice_in_dim(x, width * C, C, axis)
    smem = pl.BlockSpec(memory_space=pltpu.SMEM)
    vmem = pl.BlockSpec(memory_space=pltpu.VMEM)
    own, other = pl.pallas_call(
        lambda *refs: decode_kernel(*refs, NT=NT, HP=HP, WP=WP, FT=FT, TH=TH, TW=TW),
        out_shape=(
            jax.ShapeDtypeStruct((FT * TH, TW, C2), f32),
            jax.ShapeDtypeStruct((width_count - 1, FT * TH, TW, C2), bf16),
        ),
        in_specs=[smem, vmem, vmem, vmem, vmem, vmem, pl.BlockSpec(memory_space=pl.ANY)],
        out_specs=(vmem, vmem),
        scratch_shapes=[
            pltpu.VMEM(((NT + 2) * HP * WP, 16 * LAT), bf16),
            pltpu.VMEM((48 * LAT, 4 * C), bf16),
            pltpu.VMEM((4, NT + 2, HP, WP, C), f32),
            pltpu.VMEM((pl.cdiv(C, 128), (FT + 2) * (TH + 2), NW + 16, 128), f32),
            pltpu.VMEM((FT + 2, TH + 2, NW, 3 * C), bf16),
            pltpu.VMEM((FT * TH * NW, C2), f32),
            pltpu.VMEM(conv2_weight.shape, bf16),
            pltpu.SemaphoreType.DMA,
        ],
        compiler_params=pltpu.CompilerParams(vmem_limit_bytes=60 * 1024 * 1024),
        name="decode",
    )(
        position,
        latent,
        take(conv1_weight, 4),
        take(conv1_bias, 0)[None],
        take(norm_gain, 0)[None],
        take(norm_bias, 0)[None],
        conv2_weight,
    )
    result = own + conv2_bias
    for step in range(1, width_count):
        moved = lax.ppermute(other[step - 1], "width", [(k, (k + step) % width_count) for k in range(width_count)])
        result = result + moved.astype(f32)
    return result.reshape(FT, TH, TW, C2).astype(bf16)


def solution(mesh):
    placed = (
        P(AXES, None),
        P(),
        P(),
        P(),
        P(),
        P(),
        P(),
        P(),
        P(),
        P(None, None, None, "width", None),
        P(),
    )

    shape = (FRAMES * mesh.shape["tm"], ROWS * mesh.shape["height"], COLS * mesh.shape["width"])
    return jax.shard_map(
        lambda *args: per_device(*args, clip=shape),
        mesh=mesh,
        in_specs=placed,
        out_specs=P("tm", "height", "width", None),
        check_vma=False,
    )
```

```python
import jax
import jax.numpy as jnp
from jax import lax
from jax.experimental import pallas as pl
from jax.experimental.pallas import tpu as pltpu
from jax.sharding import PartitionSpec as P

GROUPS = 32
FRAMES = 4
ROWS = 8
COLS = 8
AXES = ("tm", "height", "width")
bf16 = jnp.bfloat16
f32 = jnp.float32


def project_kernel(tok_ref, shift_ref, scale_ref, weight_ref, bias_ref, out_ref):
    values = tok_ref[...].astype(f32)
    center = jnp.mean(values, axis=-1, keepdims=True)
    values = values - center
    spread = jnp.mean(values * values, axis=-1, keepdims=True)
    normed = (values * lax.rsqrt(spread + 1e-06) * (1.0 + scale_ref[...]) + shift_ref[...]).astype(bf16)
    patches = lax.dot_general(normed, weight_ref[...], (((1,), (1,)), ((), ())), preferred_element_type=f32)
    patches = (patches + bias_ref[...]).astype(bf16)
    size = patches.shape[1]
    lat = size // 4
    source = lax.broadcasted_iota(jnp.int32, (size, size), 0)
    target = lax.broadcasted_iota(jnp.int32, (size, size), 1)
    wanted = 4 * (target % lat) + target // lat
    order = jnp.where(source == wanted, 1.0, 0.0).astype(bf16)
    patches = jnp.dot(patches, order, preferred_element_type=f32)
    half = patches.shape[0] // 2
    packed = jnp.concatenate([patches[:half], patches[half:]], axis=1).astype(bf16)
    out_ref[...] = jnp.broadcast_to(packed[None], out_ref.shape)


def project(tokens, shift_mod, scale_mod, proj_weight, proj_bias, copies):
    count, features = tokens.shape[0], proj_weight.shape[0]
    return pl.pallas_call(
        project_kernel,
        out_shape=jax.ShapeDtypeStruct((copies, count // 2, 2 * features), bf16),
        name="project",
    )(tokens, shift_mod[None], scale_mod[None], proj_weight, proj_bias[None])


def decode_kernel(
    pos_ref,
    latent_ref,
    w1_ref,
    b1_ref,
    gain_ref,
    nbias_ref,
    w2_hbm,
    own_ref,
    other_ref,
    window,
    banded,
    hidden,
    field,
    cols,
    total,
    w2_ref,
    sem,
    *,
    NT,
    HP,
    WP,
    FT,
    TH,
    TW,
):
    C = w1_ref.shape[4]
    LAT = w1_ref.shape[3]
    C2 = w2_ref.shape[4]
    W = 2 * WP
    copy = pltpu.make_async_copy(w2_hbm, w2_ref, sem)
    copy.start()
    tm, height, width = pos_ref[0], pos_ref[1], pos_ref[2]

    for a in range(3):
        for v in range(2):
            for z in range(2):
                for i in range(2):
                    for j in range(2):
                        row = i if v == 0 else (-1 if i == 1 else 2)
                        col = j if z == 0 else (-1 if j == 1 else 2)
                        start = a * 16 * LAT + (((v * 2 + z) * 2 + i) * 2 + j) * LAT
                        for oi in range(2):
                            for oj in range(2):
                                b, e = row - oi + 1, col - oj + 1
                                at = (oi * 2 + oj) * C
                                if 0 <= b < 3 and 0 <= e < 3:
                                    banded[start : start + LAT, at : at + C] = w1_ref[a, b, e]
                                else:
                                    banded[start : start + LAT, at : at + C] = jnp.zeros((LAT, C), bf16)

    rows = latent_ref.shape[1]
    PR = rows // WP
    chunks = HP * WP // (2 * rows)
    frame_rows = HP * WP
    LN = 8 * LAT
    window[0 : 2 * frame_rows, :] = jnp.zeros((2 * frame_rows, 2 * LN), bf16)
    lane = lax.broadcasted_iota(jnp.int32, (rows, LN), 1)
    q = lax.broadcasted_iota(jnp.int32, (rows, LN), 0) % WP
    j_one = (lane // LAT) % 2 == 1
    low = lane < LN // 2
    keep = (j_one & (q > 0)) | (jnp.logical_not(j_one) & (q < WP - 1))
    i_one = (lax.broadcasted_iota(jnp.int32, (frame_rows, LN), 1) // (2 * LAT)) % 2 == 1

    def frame_body(t, carry):
        pieces = []
        for k in range(chunks):
            x = latent_ref[t * chunks + k].astype(f32)
            z = jnp.where(j_one, pltpu.roll(x, 1, 0), pltpu.roll(x, rows - 1, 0))
            z = jnp.where(keep, z, 0.0)
            zr = pltpu.roll(z, LN // 2, 1)
            xr = pltpu.roll(x, LN // 2, 1)
            pieces.append(jnp.where(low, x, zr))
            pieces.append(jnp.where(low, xr, z))
        y = jnp.concatenate(pieces, axis=0)
        zero = jnp.zeros((WP, LN), f32)
        above = jnp.concatenate([zero, y[:-WP]], axis=0)
        below = jnp.concatenate([y[WP:], zero], axis=0)
        v = jnp.where(i_one, above, below)
        base = pl.multiple_of((t + 2) * frame_rows, frame_rows)
        window[pl.ds(base, frame_rows), 0:LN] = y.astype(bf16)
        window[pl.ds(base, frame_rows), LN : 2 * LN] = v.astype(bf16)
        return carry

    lax.fori_loop(0, NT, frame_body, 0, unroll=4)

    FC = max(1, 2048 // frame_rows)
    M = FC * frame_rows
    bias = b1_ref[...]
    sums = []
    squares = []
    hidden[0:2] = jnp.zeros((2, HP, WP, 4 * C), f32)
    for n in range(4):

        def chunk_body(g, carry, n=n):
            s, sq = carry
            at = pl.multiple_of(g * M, M)
            taps = jnp.concatenate(
                [window[pl.ds(pl.multiple_of(at + a * frame_rows, frame_rows), M), :] for a in range(3)], axis=1
            )
            h = jnp.dot(taps, banded[:, n * C : (n + 1) * C], preferred_element_type=f32) + bias
            hidden[pl.ds(g * FC + 2, FC), :, :, n * C : (n + 1) * C] = h.reshape(FC, HP, WP, C)
            h8 = h.reshape(M // 8, 8, C)
            return s + jnp.sum(h8, axis=0), sq + jnp.sum(h8 * h8, axis=0)

        s, sq = lax.fori_loop(0, NT // FC, chunk_body, (jnp.zeros((8, C), f32), jnp.zeros((8, C), f32)))
        sums.append(s)
        squares.append(sq)
    s = sums[0] + sums[1] + sums[2] + sums[3]
    sq = squares[0] + squares[1] + squares[2] + squares[3]
    s = jnp.broadcast_to(jnp.sum(s, axis=0, keepdims=True), (8, C))
    sq = jnp.broadcast_to(jnp.sum(sq, axis=0, keepdims=True), (8, C))
    size = gain_ref.shape[1] * lax.axis_size("width") // GROUPS
    member = jnp.where(
        lax.broadcasted_iota(jnp.int32, (C, C), 0) // size == lax.broadcasted_iota(jnp.int32, (C, C), 1) // size, 1.0, 0.0
    )
    count = NT * HP * WP * 4 * size
    gmean = jnp.dot(s, member, preferred_element_type=f32, precision=lax.Precision.HIGHEST)[0:1] / count
    second = jnp.dot(sq, member, preferred_element_type=f32, precision=lax.Precision.HIGHEST)[0:1] / count
    gvar = second - gmean * gmean
    inverse = lax.rsqrt(gvar + 1e-06)
    gain = gain_ref[...]
    nbias = nbias_ref[...]

    R = TH + 2
    PADW = W + 16
    edge = jnp.zeros(field.shape[:2] + (1, 128), f32)
    field[:, :, 7:8, :] = edge
    field[:, :, 8 + W : 9 + W, :] = edge
    first = height * (TH // 2) - 1

    def act_body(t, carry):
        frame = tm * FT + t
        for pp in range(TH // 2 + 2):
            prow = first + pp
            source = jnp.clip(prow, 0, HP - 1)
            inside = (frame >= 2) & (prow >= 0) & (prow < HP)
            for oi in range(2):
                row = 2 * pp + oi - 1
                if row < 0 or row >= R:
                    continue
                for oj in range(2):
                    at = (oi * 2 + oj) * C
                    h = hidden[frame, source, :, at : at + C].astype(bf16).astype(f32)
                    scaled = (h - gmean) * inverse * gain + nbias
                    act = scaled / (1.0 + jnp.exp(-scaled))
                    act = jnp.where(inside, act, 0.0)
                    for plane in range(field.shape[0]):
                        part = act[:, plane * 128 : (plane + 1) * 128]
                        if C < 128:
                            part = jnp.concatenate([part, jnp.zeros((WP, 128 - C), f32)], axis=1)
                        field[plane, t * R + row, pl.ds(8 + oj, WP, stride=2), :] = part
        return carry

    lax.fori_loop(0, FT + 2, act_body, 0)

    def cols_body(t, carry):
        for r in range(R):
            for e in range(3):
                for plane in range(field.shape[0]):
                    lanes = min(C, 128)
                    at = e * C + plane * 128
                    part = field[plane, t * R + r, 7 + e : 7 + e + W, :]
                    cols[t, r, :, at : at + lanes] = part[:, :lanes].astype(bf16)
        return carry

    lax.fori_loop(0, FT + 2, cols_body, 0)

    copy.wait()
    M2 = FT * TH * W
    for a in range(3):
        for b in range(3):
            taps = cols[a : a + FT, b : b + TH].reshape(M2, 3 * C)
            part = jnp.dot(taps, w2_ref[a, b].reshape(3 * C, C2), preferred_element_type=f32)
            if a == 0 and b == 0:
                total[...] = part
            else:
                total[...] += part

    tiles = W // TW
    result = total[...].reshape(FT * TH, tiles, TW, C2)
    if tiles == 2:
        mine = width == 0
        own_ref[...] = jnp.where(mine, result[:, 0], result[:, 1])
        other_ref[0] = jnp.where(mine, result[:, 1], result[:, 0]).astype(bf16)
    else:
        for k in range(tiles):

            @pl.when(width == k)
            def _(k=k):
                own_ref[...] = result[:, k]
                for step in range(1, tiles):
                    other_ref[step - 1] = result[:, (k + step) % tiles].astype(bf16)


def per_device(
    tokens,
    shift_mod,
    scale_mod,
    proj_weight,
    proj_bias,
    conv1_weight,
    conv1_bias,
    norm_gain,
    norm_bias,
    conv2_weight,
    conv2_bias,
    *,
    clip,
):
    width_count = lax.axis_size("width")
    height_count = lax.axis_size("height")
    time_count = lax.axis_size("tm")
    devices = width_count * height_count * time_count
    NT, NH, NW = clip
    FT, TH, TW = FRAMES, ROWS, COLS
    C2 = conv2_weight.shape[4]
    HP, WP = NH // 2, NW // 2
    C = conv2_weight.shape[3]
    LAT = conv1_weight.shape[3]

    spread = project(tokens, shift_mod, scale_mod, proj_weight, proj_bias, devices)
    latent = lax.all_to_all(spread, AXES, 0, 0, tiled=True)
    latent = pltpu.with_memory_space_constraint(latent, pltpu.VMEM)

    width = lax.axis_index("width")
    position = jnp.stack([lax.axis_index("tm"), lax.axis_index("height"), width]).astype(jnp.int32)
    take = lambda x, axis: lax.dynamic_slice_in_dim(x, width * C, C, axis)
    smem = pl.BlockSpec(memory_space=pltpu.SMEM)
    vmem = pl.BlockSpec(memory_space=pltpu.VMEM)
    own, other = pl.pallas_call(
        lambda *refs: decode_kernel(*refs, NT=NT, HP=HP, WP=WP, FT=FT, TH=TH, TW=TW),
        out_shape=(
            pltpu.VMEM((FT * TH, TW, C2), f32),
            pltpu.VMEM((width_count - 1, FT * TH, TW, C2), bf16),
        ),
        in_specs=[smem, vmem, vmem, vmem, vmem, vmem, pl.BlockSpec(memory_space=pl.ANY)],
        out_specs=(vmem, vmem),
        scratch_shapes=[
            pltpu.VMEM(((NT + 2) * HP * WP, 16 * LAT), bf16),
            pltpu.VMEM((48 * LAT, 4 * C), bf16),
            pltpu.VMEM((NT + 2, HP, WP, 4 * C), f32),
            pltpu.VMEM((pl.cdiv(C, 128), (FT + 2) * (TH + 2), NW + 16, 128), f32),
            pltpu.VMEM((FT + 2, TH + 2, NW, 3 * C), bf16),
            pltpu.VMEM((FT * TH * NW, C2), f32),
            pltpu.VMEM(conv2_weight.shape, bf16),
            pltpu.SemaphoreType.DMA,
        ],
        compiler_params=pltpu.CompilerParams(vmem_limit_bytes=44 * 1024 * 1024),
        name="decode",
    )(
        position,
        latent,
        take(conv1_weight, 4),
        take(conv1_bias, 0)[None],
        take(norm_gain, 0)[None],
        take(norm_bias, 0)[None],
        conv2_weight,
    )
    result = own + conv2_bias
    for step in range(1, width_count):
        moved = lax.ppermute(other[step - 1], "width", [(k, (k + step) % width_count) for k in range(width_count)])
        result = result + moved.astype(f32)
    return result.reshape(FT, TH, TW, C2).astype(bf16)


def solution(mesh):
    placed = (
        P(AXES, None),
        P(),
        P(),
        P(),
        P(),
        P(),
        P(),
        P(),
        P(),
        P(None, None, None, "width", None),
        P(),
    )

    shape = (FRAMES * mesh.shape["tm"], ROWS * mesh.shape["height"], COLS * mesh.shape["width"])
    return jax.shard_map(
        lambda *args: per_device(*args, clip=shape),
        mesh=mesh,
        in_specs=placed,
        out_specs=P("tm", "height", "width", None),
        check_vma=False,
    )
```

```python
import jax
import jax.numpy as jnp
from jax import lax
from jax.experimental import pallas as pl
from jax.experimental.pallas import tpu as pltpu
from jax.sharding import PartitionSpec as P

GROUPS = 32
FRAMES = 4
ROWS = 8
COLS = 8
AXES = ("tm", "height", "width")
bf16 = jnp.bfloat16
f32 = jnp.float32


def project_kernel(tok_ref, shift_ref, scale_ref, weight_ref, bias_ref, out_ref):
    values = tok_ref[...].astype(f32)
    center = jnp.mean(values, axis=-1, keepdims=True)
    values = values - center
    spread = jnp.mean(values * values, axis=-1, keepdims=True)
    normed = (values * lax.rsqrt(spread + 1e-06) * (1.0 + scale_ref[...]) + shift_ref[...]).astype(bf16)
    patches = lax.dot_general(normed, weight_ref[...], (((1,), (1,)), ((), ())), preferred_element_type=f32)
    patches = (patches + bias_ref[...]).astype(bf16)
    size = patches.shape[1]
    lat = size // 4
    source = lax.broadcasted_iota(jnp.int32, (size, size), 0)
    target = lax.broadcasted_iota(jnp.int32, (size, size), 1)
    wanted = 4 * (target % lat) + target // lat
    order = jnp.where(source == wanted, 1.0, 0.0).astype(bf16)
    patches = jnp.dot(patches, order, preferred_element_type=f32)
    half = patches.shape[0] // 2
    packed = jnp.concatenate([patches[:half], patches[half:]], axis=1).astype(bf16)
    out_ref[...] = jnp.broadcast_to(packed[None], out_ref.shape)


def project(tokens, shift_mod, scale_mod, proj_weight, proj_bias, copies):
    count, features = tokens.shape[0], proj_weight.shape[0]
    return pl.pallas_call(
        project_kernel,
        out_shape=jax.ShapeDtypeStruct((copies, count // 2, 2 * features), bf16),
        name="project",
    )(tokens, shift_mod[None], scale_mod[None], proj_weight, proj_bias[None])


def prepare_kernel(w1_ref, b1_ref, gain_ref, nbias_ref, banded, affine):
    LAT, C = w1_ref.shape[3:]
    affine[0:1, :] = b1_ref[...]
    affine[1:2, :] = gain_ref[...]
    affine[2:3, :] = nbias_ref[...]

    for a in range(3):
        for v in range(2):
            for z in range(2):
                for i in range(2):
                    for j in range(2):
                        row = i if v == 0 else (-1 if i == 1 else 2)
                        col = j if z == 0 else (-1 if j == 1 else 2)
                        start = a * 16 * LAT + (((v * 2 + z) * 2 + i) * 2 + j) * LAT
                        for oi in range(2):
                            for oj in range(2):
                                b, e = row - oi + 1, col - oj + 1
                                at = (oi * 2 + oj) * C
                                if 0 <= b < 3 and 0 <= e < 3:
                                    banded[start : start + LAT, at : at + C] = w1_ref[a, b, e]
                                else:
                                    banded[start : start + LAT, at : at + C] = jnp.zeros((LAT, C), bf16)


def prepare(conv1_weight, conv1_bias, norm_gain, norm_bias):
    LAT, C = conv1_weight.shape[3:]
    vmem = pl.BlockSpec(memory_space=pltpu.VMEM)
    return pl.pallas_call(
        prepare_kernel,
        out_shape=(pltpu.VMEM((48 * LAT, 4 * C), bf16), pltpu.VMEM((3, C), f32)),
        in_specs=[vmem] * 4,
        out_specs=(vmem, vmem),
        compiler_params=pltpu.CompilerParams(vmem_limit_bytes=16 * 1024 * 1024),
        name="prepare",
    )(conv1_weight, conv1_bias[None], norm_gain[None], norm_bias[None])


def tile_products(cols, w2_ref, tile, n2, TH):
    C, C2 = w2_ref.shape[3:]
    total = None
    for a, first in enumerate((0, n2 + 1, 1)):
        for b in range(3):
            taps = cols[tile, first : first + n2, b : b + TH]
            taps = taps.reshape(n2 * TH * taps.shape[2], 3 * C)
            part = jnp.dot(taps, w2_ref[a, b].reshape(3 * C, C2), preferred_element_type=f32)
            total = part if total is None else total + part
    return total


def store_tile(total, out, n2, TH, TW):
    total = total.reshape(n2, TH, 2, TW, total.shape[-1])
    for p in range(n2):
        for k in range(2):
            out[2 * p + k] = total[p, :, k].astype(out.dtype)


def own_kernel(pos_ref, cols, w2_ref, own_ref):
    FT, TH, TW, _ = own_ref.shape
    total = tile_products(cols, w2_ref, pos_ref[2], FT // 2, TH)
    store_tile(total, own_ref, FT // 2, TH, TW)


def decode_kernel(
    pos_ref,
    latent_ref,
    banded,
    affine,
    w2_hbm,
    other_ref,
    cols,
    w2_ref,
    window,
    hidden,
    field,
    sem,
    *,
    NT,
    HP,
    WP,
    FT,
    TH,
    TW,
):
    C = w2_ref.shape[3]
    LAT = banded.shape[0] // 48
    W = 2 * WP
    tm, height, width = pos_ref[0], pos_ref[1], pos_ref[2]
    copy = pltpu.make_async_copy(w2_hbm, w2_ref, sem)
    copy.start()

    rows = latent_ref.shape[1]
    PR = rows // WP
    chunks = HP * WP // (2 * rows)
    frame_rows = HP * WP
    LN = 8 * LAT
    window[0 : 2 * frame_rows, :] = jnp.zeros((2 * frame_rows, 2 * LN), bf16)
    lane = lax.broadcasted_iota(jnp.int32, (rows, LN), 1)
    q = lax.broadcasted_iota(jnp.int32, (rows, LN), 0) % WP
    j_one = (lane // LAT) % 2 == 1
    low = lane < LN // 2
    keep = (j_one & (q > 0)) | (jnp.logical_not(j_one) & (q < WP - 1))
    i_one = (lax.broadcasted_iota(jnp.int32, (frame_rows, LN), 1) // (2 * LAT)) % 2 == 1

    def frame_body(t, carry):
        pieces = []
        for k in range(chunks):
            x = latent_ref[t * chunks + k].astype(f32)
            z = jnp.where(j_one, pltpu.roll(x, 1, 0), pltpu.roll(x, rows - 1, 0))
            z = jnp.where(keep, z, 0.0)
            zr = pltpu.roll(z, LN // 2, 1)
            xr = pltpu.roll(x, LN // 2, 1)
            pieces.append(jnp.where(low, x, zr))
            pieces.append(jnp.where(low, xr, z))
        y = jnp.concatenate(pieces, axis=0)
        zero = jnp.zeros((WP, LN), f32)
        above = jnp.concatenate([zero, y[:-WP]], axis=0)
        below = jnp.concatenate([y[WP:], zero], axis=0)
        v = jnp.where(i_one, above, below)
        base = pl.multiple_of((t + 2) * frame_rows, frame_rows)
        window[pl.ds(base, frame_rows), 0:LN] = y.astype(bf16)
        window[pl.ds(base, frame_rows), LN : 2 * LN] = v.astype(bf16)
        return carry

    lax.fori_loop(0, NT, frame_body, 0, unroll=4)

    FC = max(1, 2048 // frame_rows)
    M = FC * frame_rows
    bias = affine[0:1, :]
    sums = []
    squares = []
    hidden[0:2] = jnp.zeros((2, HP, WP, 4 * C), f32)
    for n in range(4):

        def chunk_body(g, carry, n=n):
            s, sq = carry
            at = pl.multiple_of(g * M, M)
            taps = jnp.concatenate(
                [window[pl.ds(pl.multiple_of(at + a * frame_rows, frame_rows), M), :] for a in range(3)], axis=1
            )
            h = jnp.dot(taps, banded[:, n * C : (n + 1) * C], preferred_element_type=f32) + bias
            hidden[pl.ds(g * FC + 2, FC), :, :, n * C : (n + 1) * C] = h.reshape(FC, HP, WP, C)
            h8 = h.reshape(M // 8, 8, C)
            return s + jnp.sum(h8, axis=0), sq + jnp.sum(h8 * h8, axis=0)

        s, sq = lax.fori_loop(0, NT // FC, chunk_body, (jnp.zeros((8, C), f32), jnp.zeros((8, C), f32)))
        sums.append(s)
        squares.append(sq)
    s = sums[0] + sums[1] + sums[2] + sums[3]
    sq = squares[0] + squares[1] + squares[2] + squares[3]
    s = jnp.broadcast_to(jnp.sum(s, axis=0, keepdims=True), (8, C))
    sq = jnp.broadcast_to(jnp.sum(sq, axis=0, keepdims=True), (8, C))
    size = C * lax.axis_size("width") // GROUPS
    member = jnp.where(
        lax.broadcasted_iota(jnp.int32, (C, C), 0) // size == lax.broadcasted_iota(jnp.int32, (C, C), 1) // size, 1.0, 0.0
    )
    count = NT * HP * WP * 4 * size
    gmean = jnp.dot(s, member, preferred_element_type=f32, precision=lax.Precision.HIGHEST)[0:1] / count
    second = jnp.dot(sq, member, preferred_element_type=f32, precision=lax.Precision.HIGHEST)[0:1] / count
    gvar = second - gmean * gmean
    inverse = lax.rsqrt(gvar + 1e-06)
    gain = affine[1:2, :]
    nbias = affine[2:3, :]

    R = TH + 2
    PADW = W + 16
    edge = jnp.zeros(field.shape[:2] + (1, 128), f32)
    field[:, :, 7:8, :] = edge
    field[:, :, 8 + W : 9 + W, :] = edge
    first = height * (TH // 2) - 1

    def act_body(t, carry):
        frame = tm * FT + t
        for pp in range(TH // 2 + 2):
            prow = first + pp
            source = jnp.clip(prow, 0, HP - 1)
            inside = (frame >= 2) & (prow >= 0) & (prow < HP)
            for oi in range(2):
                row = 2 * pp + oi - 1
                if row < 0 or row >= R:
                    continue
                for oj in range(2):
                    at = (oi * 2 + oj) * C
                    h = hidden[frame, source, :, at : at + C].astype(bf16).astype(f32)
                    scaled = (h - gmean) * inverse * gain + nbias
                    act = scaled / (1.0 + jnp.exp(-scaled))
                    act = jnp.where(inside, act, 0.0)
                    for plane in range(field.shape[0]):
                        part = act[:, plane * 128 : (plane + 1) * 128]
                        if C < 128:
                            part = jnp.concatenate([part, jnp.zeros((WP, 128 - C), f32)], axis=1)
                        field[plane, t * R + row, pl.ds(8 + oj, WP, stride=2), :] = part
        return carry

    lax.fori_loop(0, FT + 2, act_body, 0)

    n2 = FT // 2
    tiles = W // TW

    def pair_body(k, carry):
        t = jnp.where(k <= n2, 2 * k, 2 * (k - n2) - 1)
        for r in range(R):
            for tile in range(tiles):
                for e in range(3):
                    at = 7 + e + tile * TW
                    for plane in range(field.shape[0]):
                        lanes = min(C, 128)
                        lane_at = e * C + plane * 128
                        parts = [field[plane, (t + k2) * R + r, at : at + TW, :] for k2 in range(2)]
                        part = jnp.concatenate(parts, axis=0).astype(bf16)
                        cols[tile, k, r, :, lane_at : lane_at + lanes] = part[:, :lanes]
        return carry

    lax.fori_loop(0, 2 * n2 + 1, pair_body, 0)

    copy.wait()
    for step in range(1, tiles):
        tile = lax.rem(width + step, tiles)
        store_tile(tile_products(cols, w2_ref, tile, n2, TH), other_ref.at[step - 1], n2, TH, TW)


def per_device(
    tokens,
    shift_mod,
    scale_mod,
    proj_weight,
    proj_bias,
    conv1_weight,
    conv1_bias,
    norm_gain,
    norm_bias,
    conv2_weight,
    conv2_bias,
    *,
    clip,
):
    width_count = lax.axis_size("width")
    height_count = lax.axis_size("height")
    time_count = lax.axis_size("tm")
    devices = width_count * height_count * time_count
    NT, NH, NW = clip
    FT, TH, TW = FRAMES, ROWS, COLS
    C2 = conv2_weight.shape[4]
    HP, WP = NH // 2, NW // 2
    C = conv2_weight.shape[3]
    LAT = conv1_weight.shape[3]

    spread = project(tokens, shift_mod, scale_mod, proj_weight, proj_bias, devices)
    latent = lax.all_to_all(spread, AXES, 0, 0, tiled=True)
    latent = pltpu.with_memory_space_constraint(latent, pltpu.VMEM)

    width = lax.axis_index("width")
    position = jnp.stack([lax.axis_index("tm"), lax.axis_index("height"), width]).astype(jnp.int32)
    take = lambda x, axis: lax.dynamic_slice_in_dim(x, width * C, C, axis)
    smem = pl.BlockSpec(memory_space=pltpu.SMEM)
    vmem = pl.BlockSpec(memory_space=pltpu.VMEM)
    resident = lambda x: pltpu.with_memory_space_constraint(x, pltpu.VMEM)
    conv2_weight = pltpu.with_memory_space_constraint(conv2_weight, pltpu.HBM)
    banded, affine = prepare(
        take(conv1_weight, 4), take(conv1_bias, 0), take(norm_gain, 0), take(norm_bias, 0)
    )
    banded, affine = resident(banded), resident(affine)
    other, cols, w2 = pl.pallas_call(
        lambda *refs: decode_kernel(*refs, NT=NT, HP=HP, WP=WP, FT=FT, TH=TH, TW=TW),
        out_shape=(
            pltpu.VMEM((width_count - 1, FT, TH, TW, C2), bf16),
            pltpu.VMEM((width_count, FT + 1, TH + 2, 2 * TW, 3 * C), bf16),
            pltpu.VMEM(conv2_weight.shape, bf16),
        ),
        in_specs=[smem, vmem, vmem, vmem, pl.BlockSpec(memory_space=pl.ANY)],
        out_specs=(vmem, vmem, vmem),
        scratch_shapes=[
            pltpu.VMEM(((NT + 2) * HP * WP, 16 * LAT), bf16),
            pltpu.VMEM((NT + 2, HP, WP, 4 * C), f32),
            pltpu.VMEM((pl.cdiv(C, 128), (FT + 2) * (TH + 2), NW + 16, 128), f32),
            pltpu.SemaphoreType.DMA,
        ],
        compiler_params=pltpu.CompilerParams(vmem_limit_bytes=40 * 1024 * 1024),
        name="decode",
    )(
        position,
        latent,
        banded,
        affine,
        conv2_weight,
    )
    cols, w2 = resident(cols), resident(w2)
    moved = [
        lax.ppermute(other[step - 1], "width", [(k, (k + step) % width_count) for k in range(width_count)])
        for step in range(1, width_count)
    ]
    result = pl.pallas_call(
        own_kernel,
        out_shape=pltpu.VMEM((FT, TH, TW, C2), f32),
        in_specs=[smem, vmem, vmem],
        out_specs=vmem,
        compiler_params=pltpu.CompilerParams(vmem_limit_bytes=8 * 1024 * 1024),
        name="own",
    )(position, cols, w2)
    result = result + conv2_bias
    for part in moved:
        result = result + part.astype(f32)
    return result.astype(bf16)


def solution(mesh):
    placed = (
        P(AXES, None),
        P(),
        P(),
        P(),
        P(),
        P(),
        P(),
        P(),
        P(),
        P(None, None, None, "width", None),
        P(),
    )

    shape = (FRAMES * mesh.shape["tm"], ROWS * mesh.shape["height"], COLS * mesh.shape["width"])
    return jax.shard_map(
        lambda *args: per_device(*args, clip=shape),
        mesh=mesh,
        in_specs=placed,
        out_specs=P("tm", "height", "width", None),
        check_vma=False,
    )
```

```python
import jax
import jax.numpy as jnp
from jax import lax
from jax.experimental import pallas as pl
from jax.experimental.pallas import tpu as pltpu
from jax.sharding import PartitionSpec as P


GROUPS = 32
FRAMES = 4
ROWS = 8
COLS = 8
AXES = ("tm", "height", "width")
bf16 = jnp.bfloat16
f32 = jnp.float32


def project_kernel(tok_ref, shift_ref, scale_ref, weight_ref, bias_ref, out_ref):
    values = tok_ref[...].astype(f32)
    center = jnp.mean(values, axis=-1, keepdims=True)
    values = values - center
    spread = jnp.mean(values * values, axis=-1, keepdims=True)
    normed = (values * lax.rsqrt(spread + 1e-06) * (1.0 + scale_ref[...]) + shift_ref[...]).astype(bf16)
    patches = lax.dot_general(normed, weight_ref[...], (((1,), (1,)), ((), ())), preferred_element_type=f32)
    patches = (patches + bias_ref[...]).astype(bf16)
    size = patches.shape[1]
    lat = size // 4
    source = lax.broadcasted_iota(jnp.int32, (size, size), 0)
    target = lax.broadcasted_iota(jnp.int32, (size, size), 1)
    wanted = 4 * (target % lat) + target // lat
    order = jnp.where(source == wanted, 1.0, 0.0).astype(bf16)
    patches = jnp.dot(patches, order, preferred_element_type=f32)
    half = patches.shape[0] // 2
    packed = jnp.concatenate([patches[:half], patches[half:]], axis=1).astype(bf16)
    out_ref[...] = jnp.broadcast_to(packed[None], out_ref.shape)


def project(tokens, shift_mod, scale_mod, proj_weight, proj_bias, copies):
    count, features = tokens.shape[0], proj_weight.shape[0]
    operands = (tokens, shift_mod[None], scale_mod[None], proj_weight, proj_bias[None])
    return pl.pallas_call(
        project_kernel,
        out_shape=pltpu.VMEM((copies, count // 2, 2 * features), bf16),
        compiler_params=pltpu.CompilerParams(vmem_limit_bytes=16 * 1024 * 1024),
        name="project",
    )(*[pltpu.with_memory_space_constraint(x, pltpu.HBM) for x in operands])


def prepare_kernel(w1_ref, b1_ref, gain_ref, nbias_ref, banded, affine):
    LAT, C = w1_ref.shape[3:]
    affine[0:1, :] = b1_ref[...]
    affine[1:2, :] = gain_ref[...]
    affine[2:3, :] = nbias_ref[...]

    for a in range(3):
        for v in range(2):
            for z in range(2):
                for i in range(2):
                    for j in range(2):
                        row = i if v == 0 else (-1 if i == 1 else 2)
                        col = j if z == 0 else (-1 if j == 1 else 2)
                        start = a * 16 * LAT + (((v * 2 + z) * 2 + i) * 2 + j) * LAT
                        for oi in range(2):
                            for oj in range(2):
                                b, e = row - oi + 1, col - oj + 1
                                at = (oi * 2 + oj) * C
                                if 0 <= b < 3 and 0 <= e < 3:
                                    banded[start : start + LAT, at : at + C] = w1_ref[a, b, e]
                                else:
                                    banded[start : start + LAT, at : at + C] = jnp.zeros((LAT, C), bf16)


def prepare(conv1_weight, conv1_bias, norm_gain, norm_bias):
    LAT, C = conv1_weight.shape[3:]
    vmem = pl.BlockSpec(memory_space=pltpu.VMEM)
    return pl.pallas_call(
        prepare_kernel,
        out_shape=(pltpu.VMEM((48 * LAT, 4 * C), bf16), pltpu.VMEM((3, C), f32)),
        in_specs=[vmem] * 4,
        out_specs=(vmem, vmem),
        compiler_params=pltpu.CompilerParams(vmem_limit_bytes=16 * 1024 * 1024),
        name="prepare",
    )(conv1_weight, conv1_bias[None], norm_gain[None], norm_bias[None])


def tile_products(cols, w2_ref, tile, n2, TH, low, high):
    C = w2_ref.shape[3]
    total = None
    for a, first in enumerate((0, n2 + 1, 1)):
        for b in range(3):
            taps = cols[tile, first : first + n2, b : b + TH]
            taps = taps.reshape(n2 * TH * taps.shape[2], 3 * C)
            part = jnp.dot(taps, w2_ref[a, b, :, :, low:high].reshape(3 * C, high - low), preferred_element_type=f32)
            total = part if total is None else total + part
    return total


def store_tile(total, out, n2, TH, TW):
    total = total.reshape(n2, TH, 2, TW, total.shape[-1])
    for p in range(n2):
        for k in range(2):
            out[2 * p + k] = total[p, :, k].astype(out.dtype)


def send_tiles(cols, w2_ref, width, other_ref, low):
    steps, FT, TH, TW, span = other_ref.shape
    for step in range(steps):
        tile = lax.rem(width + step + 1, steps + 1)
        total = tile_products(cols, w2_ref, tile, FT // 2, TH, low, low + span)
        store_tile(total, other_ref.at[step], FT // 2, TH, TW)


def send_kernel(pos_ref, cols, w2_ref, other_ref, *, low):
    send_tiles(cols, w2_ref, pos_ref[2], other_ref, low)


def own_kernel(pos_ref, cols, w2_ref, own_ref):
    FT, TH, TW, _ = own_ref.shape
    total = tile_products(cols, w2_ref, pos_ref[2], FT // 2, TH, 0, own_ref.shape[3])
    store_tile(total, own_ref, FT // 2, TH, TW)


def decode_kernel(
    pos_ref,
    latent_ref,
    banded,
    affine,
    w2_hbm,
    other_ref,
    cols,
    w2_ref,
    window,
    hidden,
    field,
    sem,
    *,
    NT,
    HP,
    WP,
    FT,
    TH,
    TW,
):
    C = w2_ref.shape[3]
    LAT = banded.shape[0] // 48
    W = 2 * WP
    tm, height, width = pos_ref[0], pos_ref[1], pos_ref[2]
    copy = pltpu.make_async_copy(w2_hbm, w2_ref, sem)
    copy.start()

    rows = latent_ref.shape[1]
    chunks = HP * WP // (2 * rows)
    frame_rows = HP * WP
    LN = 8 * LAT
    window[0 : 2 * frame_rows, :] = jnp.zeros((2 * frame_rows, 2 * LN), bf16)
    lane = lax.broadcasted_iota(jnp.int32, (rows, LN), 1)
    q = lax.broadcasted_iota(jnp.int32, (rows, LN), 0) % WP
    j_one = (lane // LAT) % 2 == 1
    low = lane < LN // 2
    keep = (j_one & (q > 0)) | (jnp.logical_not(j_one) & (q < WP - 1))
    i_one = (lax.broadcasted_iota(jnp.int32, (frame_rows, LN), 1) // (2 * LAT)) % 2 == 1

    def frame_body(t, carry):
        pieces = []
        for k in range(chunks):
            x = latent_ref[t * chunks + k].astype(f32)
            z = jnp.where(j_one, pltpu.roll(x, 1, 0), pltpu.roll(x, rows - 1, 0))
            z = jnp.where(keep, z, 0.0)
            zr = pltpu.roll(z, LN // 2, 1)
            xr = pltpu.roll(x, LN // 2, 1)
            pieces.append(jnp.where(low, x, zr))
            pieces.append(jnp.where(low, xr, z))
        y = jnp.concatenate(pieces, axis=0)
        zero = jnp.zeros((WP, LN), f32)
        above = jnp.concatenate([zero, y[:-WP]], axis=0)
        below = jnp.concatenate([y[WP:], zero], axis=0)
        v = jnp.where(i_one, above, below)
        base = pl.multiple_of((t + 2) * frame_rows, frame_rows)
        window[pl.ds(base, frame_rows), 0:LN] = y.astype(bf16)
        window[pl.ds(base, frame_rows), LN : 2 * LN] = v.astype(bf16)
        return carry

    lax.fori_loop(0, NT, frame_body, 0, unroll=4)

    FC = max(1, 2048 // frame_rows)
    M = FC * frame_rows
    bias = affine[0:1, :]
    sums = []
    squares = []
    hidden[0:2] = jnp.zeros((2, HP, WP, 4 * C), f32)
    for n in range(4):

        def chunk_body(g, carry, n=n):
            s, sq = carry
            at = pl.multiple_of(g * M, M)
            taps = jnp.concatenate(
                [window[pl.ds(pl.multiple_of(at + a * frame_rows, frame_rows), M), :] for a in range(3)], axis=1
            )
            h = jnp.dot(taps, banded[:, n * C : (n + 1) * C], preferred_element_type=f32) + bias
            hidden[pl.ds(g * FC + 2, FC), :, :, n * C : (n + 1) * C] = h.reshape(FC, HP, WP, C)
            h8 = h.reshape(M // 8, 8, C)
            return s + jnp.sum(h8, axis=0), sq + jnp.sum(h8 * h8, axis=0)

        s, sq = lax.fori_loop(0, NT // FC, chunk_body, (jnp.zeros((8, C), f32), jnp.zeros((8, C), f32)))
        sums.append(s)
        squares.append(sq)
    s = sums[0] + sums[1] + sums[2] + sums[3]
    sq = squares[0] + squares[1] + squares[2] + squares[3]
    s = jnp.broadcast_to(jnp.sum(s, axis=0, keepdims=True), (8, C))
    sq = jnp.broadcast_to(jnp.sum(sq, axis=0, keepdims=True), (8, C))
    size = C * lax.axis_size("width") // GROUPS
    member = jnp.where(
        lax.broadcasted_iota(jnp.int32, (C, C), 0) // size == lax.broadcasted_iota(jnp.int32, (C, C), 1) // size, 1.0, 0.0
    )
    count = NT * HP * WP * 4 * size
    gmean = jnp.dot(s, member, preferred_element_type=f32, precision=lax.Precision.HIGHEST)[0:1] / count
    second = jnp.dot(sq, member, preferred_element_type=f32, precision=lax.Precision.HIGHEST)[0:1] / count
    gvar = second - gmean * gmean
    inverse = lax.rsqrt(gvar + 1e-06)
    slope = 0.5 * inverse * affine[1:2, :]
    offset = 0.5 * affine[2:3, :]

    R = TH + 2
    edge = jnp.zeros(field.shape[:2] + (1, 128), f32)
    field[:, :, 7:8, :] = edge
    field[:, :, 8 + W : 9 + W, :] = edge
    first = height * (TH // 2) - 1

    def act_body(t, carry):
        frame = tm * FT + t
        for pp in range(TH // 2 + 2):
            prow = first + pp
            source = jnp.clip(prow, 0, HP - 1)
            inside = (frame >= 2) & (prow >= 0) & (prow < HP)
            for oi in range(2):
                row = 2 * pp + oi - 1
                if row < 0 or row >= R:
                    continue
                for oj in range(2):
                    at = (oi * 2 + oj) * C
                    h = hidden[frame, source, :, at : at + C].astype(bf16).astype(f32)
                    half = (h - gmean) * slope + offset
                    act = half * jnp.tanh(half) + half
                    act = jnp.where(inside, act, 0.0)
                    for plane in range(field.shape[0]):
                        part = act[:, plane * 128 : (plane + 1) * 128]
                        if C < 128:
                            part = jnp.concatenate([part, jnp.zeros((WP, 128 - C), f32)], axis=1)
                        field[plane, t * R + row, pl.ds(8 + oj, WP, stride=2), :] = part
        return carry

    lax.fori_loop(0, FT + 2, act_body, 0)

    n2 = FT // 2
    tiles = W // TW

    def pair_body(k, carry):
        t = jnp.where(k <= n2, 2 * k, 2 * (k - n2) - 1)
        for r in range(R):
            for tile in range(tiles):
                for e in range(3):
                    at = 7 + e + tile * TW
                    for plane in range(field.shape[0]):
                        lanes = min(C, 128)
                        lane_at = e * C + plane * 128
                        parts = [field[plane, (t + k2) * R + r, at : at + TW, :] for k2 in range(2)]
                        part = jnp.concatenate(parts, axis=0).astype(bf16)
                        cols[tile, k, r, :, lane_at : lane_at + lanes] = part[:, :lanes]
        return carry

    lax.fori_loop(0, 2 * n2 + 1, pair_body, 0)

    copy.wait()

    def once(k, carry):
        send_tiles(cols, w2_ref, width + k, other_ref, 0)
        return carry

    lax.fori_loop(0, jnp.minimum(width + 1, 1), once, 0)


def decode(
    tokens,
    shift_mod,
    scale_mod,
    proj_weight,
    proj_bias,
    conv1_weight,
    conv1_bias,
    norm_gain,
    norm_bias,
    conv2_weight,
    conv2_bias,
    *,
    clip,
):
    width_count = lax.axis_size("width")
    height_count = lax.axis_size("height")
    time_count = lax.axis_size("tm")
    devices = width_count * height_count * time_count
    NT, NH, NW = clip
    FT, TH, TW = FRAMES, ROWS, COLS
    C2 = conv2_weight.shape[4]
    HP, WP = NH // 2, NW // 2
    C = conv2_weight.shape[3]
    LAT = conv1_weight.shape[3]

    spread = project(tokens, shift_mod, scale_mod, proj_weight, proj_bias, devices)
    latent = lax.all_to_all(spread, AXES, 0, 0, tiled=True)
    latent = pltpu.with_memory_space_constraint(latent, pltpu.VMEM)

    width = lax.axis_index("width")
    position = jnp.stack([lax.axis_index("tm"), lax.axis_index("height"), width]).astype(jnp.int32)
    take = lambda x, axis: lax.dynamic_slice_in_dim(x, width * C, C, axis)
    smem = pl.BlockSpec(memory_space=pltpu.SMEM)
    vmem = pl.BlockSpec(memory_space=pltpu.VMEM)
    resident = lambda x: pltpu.with_memory_space_constraint(x, pltpu.VMEM)
    conv2_weight = pltpu.with_memory_space_constraint(conv2_weight, pltpu.HBM)
    banded, affine = prepare(
        take(conv1_weight, 4), take(conv1_bias, 0), take(norm_gain, 0), take(norm_bias, 0)
    )
    banded, affine = resident(banded), resident(affine)
    span = C2 // 2
    sent = pltpu.VMEM((width_count - 1, FT, TH, TW, span), bf16)
    other, cols, w2 = pl.pallas_call(
        lambda *refs: decode_kernel(*refs, NT=NT, HP=HP, WP=WP, FT=FT, TH=TH, TW=TW),
        out_shape=(
            sent,
            pltpu.VMEM((width_count, FT + 1, TH + 2, 2 * TW, 3 * C), bf16),
            pltpu.VMEM(conv2_weight.shape, bf16),
        ),
        in_specs=[smem, vmem, vmem, vmem, pl.BlockSpec(memory_space=pl.ANY)],
        out_specs=(vmem, vmem, vmem),
        scratch_shapes=[
            pltpu.VMEM(((NT + 2) * HP * WP, 16 * LAT), bf16),
            pltpu.VMEM((NT + 2, HP, WP, 4 * C), f32),
            pltpu.VMEM((pl.cdiv(C, 128), (FT + 2) * (TH + 2), NW + 16, 128), f32),
            pltpu.SemaphoreType.DMA,
        ],
        compiler_params=pltpu.CompilerParams(vmem_limit_bytes=40 * 1024 * 1024),
        name="decode",
    )(
        position,
        latent,
        banded,
        affine,
        conv2_weight,
    )
    cols, w2 = resident(cols), resident(w2)

    def exchange(other):
        return [
            lax.ppermute(other[step - 1], "width", [(k, (k + step) % width_count) for k in range(width_count)])
            for step in range(1, width_count)
        ]

    def send(low):
        return pl.pallas_call(
            lambda *refs: send_kernel(*refs, low=low),
            out_shape=sent,
            in_specs=[smem, vmem, vmem],
            out_specs=vmem,
            compiler_params=pltpu.CompilerParams(vmem_limit_bytes=8 * 1024 * 1024),
            name="send",
        )(position, cols, w2)

    moved_low = exchange(other)
    other = send(span)
    moved_high = exchange(other)
    result = pl.pallas_call(
        own_kernel,
        out_shape=pltpu.VMEM((FT, TH, TW, C2), f32),
        in_specs=[smem, vmem, vmem],
        out_specs=vmem,
        compiler_params=pltpu.CompilerParams(vmem_limit_bytes=8 * 1024 * 1024),
        name="own",
    )(position, cols, w2)
    result = result + conv2_bias
    for low, high in zip(moved_low, moved_high):
        result = result + jnp.concatenate([low, high], axis=-1).astype(f32)
    return result.astype(bf16)


def solution(mesh):
    placed = (
        P(AXES, None),
        P(),
        P(),
        P(),
        P(),
        P(),
        P(),
        P(),
        P(),
        P(None, None, None, "width", None),
        P(),
    )

    shape = (FRAMES * mesh.shape["tm"], ROWS * mesh.shape["height"], COLS * mesh.shape["width"])
    return jax.shard_map(
        lambda *args: decode(*args, clip=shape),
        mesh=mesh,
        in_specs=placed,
        out_specs=P("tm", "height", "width", None),
        check_vma=False,
    )
```

```python
import jax
import jax.numpy as jnp
from jax import lax
from jax.experimental import pallas as pl
from jax.experimental.pallas import tpu as pltpu
from jax.sharding import PartitionSpec as P


GROUPS = 32
FRAMES = 4
ROWS = 8
COLS = 8
AXES = ("ty", "tc", "height", "width")
TIME = ("ty", "tc")
bf16 = jnp.bfloat16
f32 = jnp.float32


def project_kernel(tok_ref, shift_ref, scale_ref, weight_ref, bias_ref, out_ref):
    values = tok_ref[...].astype(f32)
    center = jnp.mean(values, axis=-1, keepdims=True)
    values = values - center
    spread = jnp.mean(values * values, axis=-1, keepdims=True)
    normed = (values * lax.rsqrt(spread + 1e-06) * (1.0 + scale_ref[...]) + shift_ref[...]).astype(bf16)
    patches = lax.dot_general(normed, weight_ref[...], (((1,), (1,)), ((), ())), preferred_element_type=f32)
    patches = (patches + bias_ref[...]).astype(bf16)
    size = patches.shape[1]
    lat = size // 4
    source = lax.broadcasted_iota(jnp.int32, (size, size), 0)
    target = lax.broadcasted_iota(jnp.int32, (size, size), 1)
    wanted = 4 * (target % lat) + target // lat
    order = jnp.where(source == wanted, 1.0, 0.0).astype(bf16)
    patches = jnp.dot(patches, order, preferred_element_type=f32)
    half = patches.shape[0] // 2
    packed = jnp.concatenate([patches[:half], patches[half:]], axis=1).astype(bf16)
    out_ref[...] = jnp.broadcast_to(packed[None], out_ref.shape)


def project(tokens, shift_mod, scale_mod, proj_weight, proj_bias, copies):
    count, features = tokens.shape[0], proj_weight.shape[0]
    operands = (tokens, shift_mod[None], scale_mod[None], proj_weight, proj_bias[None])
    return pl.pallas_call(
        project_kernel,
        out_shape=pltpu.VMEM((copies, count // 2, 2 * features), bf16),
        compiler_params=pltpu.CompilerParams(vmem_limit_bytes=16 * 1024 * 1024),
        name="project",
    )(*[pltpu.with_memory_space_constraint(x, pltpu.HBM) for x in operands])


def prepare_kernel(w1_ref, b1_ref, gain_ref, nbias_ref, banded, affine):
    LAT, C = w1_ref.shape[3:]
    affine[0:1, :] = b1_ref[...]
    affine[1:2, :] = gain_ref[...]
    affine[2:3, :] = nbias_ref[...]

    for a in range(3):
        for v in range(2):
            for z in range(2):
                for i in range(2):
                    for j in range(2):
                        row = i if v == 0 else (-1 if i == 1 else 2)
                        col = j if z == 0 else (-1 if j == 1 else 2)
                        start = a * 16 * LAT + (((v * 2 + z) * 2 + i) * 2 + j) * LAT
                        for oi in range(2):
                            for oj in range(2):
                                b, e = row - oi + 1, col - oj + 1
                                at = (oi * 2 + oj) * C
                                if 0 <= b < 3 and 0 <= e < 3:
                                    banded[start : start + LAT, at : at + C] = w1_ref[a, b, e]
                                else:
                                    banded[start : start + LAT, at : at + C] = jnp.zeros((LAT, C), bf16)


def prepare(conv1_weight, conv1_bias, norm_gain, norm_bias):
    LAT, C = conv1_weight.shape[3:]
    vmem = pl.BlockSpec(memory_space=pltpu.VMEM)
    return pl.pallas_call(
        prepare_kernel,
        out_shape=(pltpu.VMEM((48 * LAT, 4 * C), bf16), pltpu.VMEM((3, C), f32)),
        in_specs=[vmem] * 4,
        out_specs=(vmem, vmem),
        compiler_params=pltpu.CompilerParams(vmem_limit_bytes=16 * 1024 * 1024),
        name="prepare",
    )(conv1_weight, conv1_bias[None], norm_gain[None], norm_bias[None])


def tile_products(cols, w2_ref, tile, n2, TH, low, high):
    C = w2_ref.shape[3]
    total = None
    for a, first in enumerate((0, n2 + 1, 1)):
        for b in range(3):
            taps = cols[tile, first : first + n2, b : b + TH]
            taps = taps.reshape(n2 * TH * taps.shape[2], 3 * C)
            part = jnp.dot(taps, w2_ref[a, b, :, :, low:high].reshape(3 * C, high - low), preferred_element_type=f32)
            total = part if total is None else total + part
    return total


def store_tile(total, out, n2, TH, TW):
    total = total.reshape(n2, TH, 2, TW, total.shape[-1])
    for p in range(n2):
        for k in range(2):
            out[2 * p + k] = total[p, :, k].astype(out.dtype)


def send_tiles(cols, w2_ref, width, other_ref, low):
    steps, FT, TH, TW, span = other_ref.shape
    for step in range(steps):
        tile = lax.rem(width + step + 1, steps + 1)
        total = tile_products(cols, w2_ref, tile, FT // 2, TH, low, low + span)
        store_tile(total, other_ref.at[step], FT // 2, TH, TW)


def send_kernel(pos_ref, cols, w2_ref, other_ref, *, low):
    send_tiles(cols, w2_ref, pos_ref[2], other_ref, low)


def own_kernel(pos_ref, cols, w2_ref, own_ref):
    FT, TH, TW, _ = own_ref.shape
    total = tile_products(cols, w2_ref, pos_ref[2], FT // 2, TH, 0, own_ref.shape[3])
    store_tile(total, own_ref, FT // 2, TH, TW)


def window_writer(rows, HP, WP, LAT):
    frame_rows = HP * WP
    LN = 8 * LAT
    lane = lax.broadcasted_iota(jnp.int32, (rows, LN), 1)
    q = lax.broadcasted_iota(jnp.int32, (rows, LN), 0) % WP
    j_one = (lane // LAT) % 2 == 1
    low = lane < LN // 2
    keep = (j_one & (q > 0)) | (jnp.logical_not(j_one) & (q < WP - 1))
    i_one = (lax.broadcasted_iota(jnp.int32, (frame_rows, LN), 1) // (2 * LAT)) % 2 == 1

    def write(window, slot, latent_ref, first):
        pieces = []
        for k in range(frame_rows // (2 * rows)):
            x = latent_ref[first + k].astype(f32)
            z = jnp.where(j_one, pltpu.roll(x, 1, 0), pltpu.roll(x, rows - 1, 0))
            z = jnp.where(keep, z, 0.0)
            zr = pltpu.roll(z, LN // 2, 1)
            xr = pltpu.roll(x, LN // 2, 1)
            pieces.append(jnp.where(low, x, zr))
            pieces.append(jnp.where(low, xr, z))
        y = jnp.concatenate(pieces, axis=0)
        zero = jnp.zeros((WP, LN), f32)
        above = jnp.concatenate([zero, y[:-WP]], axis=0)
        below = jnp.concatenate([y[WP:], zero], axis=0)
        v = jnp.where(i_one, above, below)
        window[slot, :, 0:LN] = y.astype(bf16)
        window[slot, :, LN : 2 * LN] = v.astype(bf16)

    return write


def hidden_frames(frames, banded, bias, out, first, sums):
    C = bias.shape[1]
    s, sq = sums
    for n in range(4):
        taps = jnp.concatenate(
            [jnp.concatenate([frame[a]() for frame in frames], axis=0) for a in range(3)], axis=1
        )
        h = jnp.dot(taps, banded[:, n * C : (n + 1) * C], preferred_element_type=f32) + bias
        out[first : first + len(frames), :, :, n * C : (n + 1) * C] = h.reshape((len(frames),) + out.shape[1:3] + (C,))
        h8 = h.reshape(h.shape[0] // 8, 8, C)
        s = s + jnp.sum(h8, axis=0)
        sq = sq + jnp.sum(h8 * h8, axis=0)
    return s, sq


def loader(window, slot):
    return lambda: window[slot]


def early_kernel(mine_ref, banded, affine, window, hidden, sums, *, HP, WP, FT):
    TY = (window.shape[0] - 2) // FT
    chunks = mine_ref.shape[0] // (TY * FT)
    C = affine.shape[1]
    write = window_writer(mine_ref.shape[1], HP, WP, banded.shape[0] // 48)
    window[TY * FT :] = jnp.zeros((2,) + window.shape[1:], bf16)
    totals = (jnp.zeros((8, C), f32), jnp.zeros((8, C), f32))
    for ty in range(TY):
        for k in range(FT):
            write(window, ty * FT + k, mine_ref, (ty * FT + k) * chunks)
    for ty in range(TY):
        frames = [[loader(window, ty * FT + k + a - 2) for a in range(3)] for k in range(2, FT)]
        totals = hidden_frames(frames, banded, affine[0:1, :], hidden, ty * (FT - 2), totals)
    sums[0:8, :] = totals[0]
    sums[8:16, :] = totals[1]


def decode_kernel(
    pos_ref,
    theirs_ref,
    window_mine,
    hidden_early,
    sums_early,
    banded,
    affine,
    w2_hbm,
    other_ref,
    cols,
    w2_ref,
    window,
    hidden,
    field,
    sem,
    *,
    NT,
    HP,
    WP,
    FT,
    TH,
    TW,
):
    C = w2_ref.shape[3]
    W = 2 * WP
    tm, height, width = pos_ref[0], pos_ref[1], pos_ref[2]
    tc = tm % 2
    copy = pltpu.make_async_copy(w2_hbm, w2_ref, sem)
    copy.start()

    TY = NT // (2 * FT)
    chunks = theirs_ref.shape[0] // (TY * FT)
    write = window_writer(theirs_ref.shape[1], HP, WP, banded.shape[0] // 48)
    window[TY * FT :] = jnp.zeros((2,) + window.shape[1:], bf16)
    for ty in range(TY):
        for k in range(FT):
            write(window, ty * FT + k, theirs_ref, (ty * FT + k) * chunks)

    s, sq = sums_early[0:8, :], sums_early[8:16, :]
    for ty in range(TY):
        same = ty * FT + FT - 2
        previous = (ty - 1) * FT + FT - 2 if ty > 0 else TY * FT
        before_mine = jnp.where(tc == 1, same, previous)
        before_theirs = jnp.where(tc == 1, previous, same)
        sequence_mine = [loader(window, before_mine + k) for k in range(2)]
        sequence_mine += [loader(window_mine, ty * FT + k) for k in range(2)]
        sequence_theirs = [loader(window_mine, before_theirs + k) for k in range(2)]
        sequence_theirs += [loader(window, ty * FT + k) for k in range(FT)]
        frames = [sequence_theirs[k : k + 3] for k in reversed(range(FT))] + [sequence_mine[k : k + 3] for k in range(2)]
        s, sq = hidden_frames(frames, banded, affine[0:1, :], hidden, ty * (FT + 2), (s, sq))
    s = jnp.broadcast_to(jnp.sum(s, axis=0, keepdims=True), (8, C))
    sq = jnp.broadcast_to(jnp.sum(sq, axis=0, keepdims=True), (8, C))
    size = C * lax.axis_size("width") // GROUPS
    member = jnp.where(
        lax.broadcasted_iota(jnp.int32, (C, C), 0) // size == lax.broadcasted_iota(jnp.int32, (C, C), 1) // size, 1.0, 0.0
    )
    count = NT * HP * WP * 4 * size
    gmean = jnp.dot(s, member, preferred_element_type=f32, precision=lax.Precision.HIGHEST)[0:1] / count
    second = jnp.dot(sq, member, preferred_element_type=f32, precision=lax.Precision.HIGHEST)[0:1] / count
    gvar = second - gmean * gmean
    inverse = lax.rsqrt(gvar + 1e-06)
    slope = 0.5 * inverse * affine[1:2, :]
    offset = 0.5 * affine[2:3, :]

    R = TH + 2
    edge = jnp.zeros(field.shape[:2] + (1, 128), f32)
    field[:, :, 7:8, :] = edge
    field[:, :, 8 + W : 9 + W, :] = edge
    first = height * (TH // 2) - 1

    def act_body(t, carry):
        actual = tm * FT + t - 2
        frame = jnp.maximum(actual, 0)
        group, k = frame // FT, frame % FT
        mine = group % 2 == tc
        early = mine & (k >= 2)
        slot_early = (group // 2) * (FT - 2) + jnp.maximum(k - 2, 0)
        slot = (group // 2) * (FT + 2) + jnp.where(mine, FT + jnp.minimum(k, 1), FT - 1 - k)
        for pp in range(TH // 2 + 2):
            prow = first + pp
            source = jnp.clip(prow, 0, HP - 1)
            inside = (actual >= 0) & (prow >= 0) & (prow < HP)
            for oi in range(2):
                row = 2 * pp + oi - 1
                if row < 0 or row >= R:
                    continue
                for oj in range(2):
                    at = (oi * 2 + oj) * C
                    h = jnp.where(
                        early, hidden_early[slot_early, source, :, at : at + C], hidden[slot, source, :, at : at + C]
                    )
                    h = h.astype(bf16).astype(f32)
                    half = (h - gmean) * slope + offset
                    act = half * jnp.tanh(half) + half
                    act = jnp.where(inside, act, 0.0)
                    for plane in range(field.shape[0]):
                        part = act[:, plane * 128 : (plane + 1) * 128]
                        if C < 128:
                            part = jnp.concatenate([part, jnp.zeros((WP, 128 - C), f32)], axis=1)
                        field[plane, t * R + row, pl.ds(8 + oj, WP, stride=2), :] = part
        return carry

    lax.fori_loop(0, FT + 2, act_body, 0)

    n2 = FT // 2
    tiles = W // TW

    def pair_body(k, carry):
        t = jnp.where(k <= n2, 2 * k, 2 * (k - n2) - 1)
        for r in range(R):
            for tile in range(tiles):
                for e in range(3):
                    at = 7 + e + tile * TW
                    for plane in range(field.shape[0]):
                        lanes = min(C, 128)
                        lane_at = e * C + plane * 128
                        parts = [field[plane, (t + k2) * R + r, at : at + TW, :] for k2 in range(2)]
                        part = jnp.concatenate(parts, axis=0).astype(bf16)
                        cols[tile, k, r, :, lane_at : lane_at + lanes] = part[:, :lanes]
        return carry

    lax.fori_loop(0, 2 * n2 + 1, pair_body, 0)

    copy.wait()

    def once(k, carry):
        send_tiles(cols, w2_ref, width + k, other_ref, 0)
        return carry

    lax.fori_loop(0, jnp.minimum(width + 1, 1), once, 0)


def decode(
    tokens,
    shift_mod,
    scale_mod,
    proj_weight,
    proj_bias,
    conv1_weight,
    conv1_bias,
    norm_gain,
    norm_bias,
    conv2_weight,
    conv2_bias,
    *,
    clip,
):
    width_count = lax.axis_size("width")
    height_count = lax.axis_size("height")
    time_count = lax.axis_size(TIME)
    devices = width_count * height_count * time_count
    NT, NH, NW = clip
    FT, TH, TW = FRAMES, ROWS, COLS
    C2 = conv2_weight.shape[4]
    HP, WP = NH // 2, NW // 2
    C = conv2_weight.shape[3]
    LAT = conv1_weight.shape[3]

    spread = project(tokens, shift_mod, scale_mod, proj_weight, proj_bias, devices // 2)
    mine = lax.all_to_all(spread, ("ty", "height", "width"), 0, 0, tiled=True)
    theirs = lax.ppermute(mine, "tc", [(0, 1), (1, 0)])

    width = lax.axis_index("width")
    position = jnp.stack([lax.axis_index(TIME), lax.axis_index("height"), width]).astype(jnp.int32)
    take = lambda x, axis: lax.dynamic_slice_in_dim(x, width * C, C, axis)
    smem = pl.BlockSpec(memory_space=pltpu.SMEM)
    vmem = pl.BlockSpec(memory_space=pltpu.VMEM)
    resident = lambda x: pltpu.with_memory_space_constraint(x, pltpu.VMEM)
    conv2_weight = pltpu.with_memory_space_constraint(conv2_weight, pltpu.HBM)
    mine, theirs = resident(mine), resident(theirs)
    banded, affine = prepare(
        take(conv1_weight, 4), take(conv1_bias, 0), take(norm_gain, 0), take(norm_bias, 0)
    )
    banded, affine = resident(banded), resident(affine)
    TY = time_count // 2
    window, hidden, sums = pl.pallas_call(
        lambda *refs: early_kernel(*refs, HP=HP, WP=WP, FT=FT),
        out_shape=(
            pltpu.VMEM((TY * FT + 2, HP * WP, 16 * LAT), bf16),
            pltpu.VMEM((TY * (FT - 2), HP, WP, 4 * C), f32),
            pltpu.VMEM((16, C), f32),
        ),
        in_specs=[vmem, vmem, vmem],
        out_specs=(vmem, vmem, vmem),
        compiler_params=pltpu.CompilerParams(vmem_limit_bytes=12 * 1024 * 1024),
        name="early",
    )(mine, banded, affine)
    window, hidden, sums = resident(window), resident(hidden), resident(sums)
    span = C2 // 2
    sent = pltpu.VMEM((width_count - 1, FT, TH, TW, span), bf16)
    other, cols, w2 = pl.pallas_call(
        lambda *refs: decode_kernel(*refs, NT=NT, HP=HP, WP=WP, FT=FT, TH=TH, TW=TW),
        out_shape=(
            sent,
            pltpu.VMEM((width_count, FT + 1, TH + 2, 2 * TW, 3 * C), bf16),
            pltpu.VMEM(conv2_weight.shape, bf16),
        ),
        in_specs=[smem] + [vmem] * 6 + [pl.BlockSpec(memory_space=pl.ANY)],
        out_specs=(vmem, vmem, vmem),
        scratch_shapes=[
            pltpu.VMEM((TY * FT + 2, HP * WP, 16 * LAT), bf16),
            pltpu.VMEM((TY * (FT + 2), HP, WP, 4 * C), f32),
            pltpu.VMEM((pl.cdiv(C, 128), (FT + 2) * (TH + 2), NW + 16, 128), f32),
            pltpu.SemaphoreType.DMA,
        ],
        compiler_params=pltpu.CompilerParams(vmem_limit_bytes=28 * 1024 * 1024),
        name="decode",
    )(position, theirs, window, hidden, sums, banded, affine, conv2_weight)
    cols, w2 = resident(cols), resident(w2)

    def exchange(other):
        return [
            lax.ppermute(other[step - 1], "width", [(k, (k + step) % width_count) for k in range(width_count)])
            for step in range(1, width_count)
        ]

    def send(low):
        return pl.pallas_call(
            lambda *refs: send_kernel(*refs, low=low),
            out_shape=sent,
            in_specs=[smem, vmem, vmem],
            out_specs=vmem,
            compiler_params=pltpu.CompilerParams(vmem_limit_bytes=8 * 1024 * 1024),
            name="send",
        )(position, cols, w2)

    moved_low = exchange(other)
    other = send(span)
    moved_high = exchange(other)
    result = pl.pallas_call(
        own_kernel,
        out_shape=pltpu.VMEM((FT, TH, TW, C2), f32),
        in_specs=[smem, vmem, vmem],
        out_specs=vmem,
        compiler_params=pltpu.CompilerParams(vmem_limit_bytes=8 * 1024 * 1024),
        name="own",
    )(position, cols, w2)
    result = result + conv2_bias
    for low, high in zip(moved_low, moved_high):
        result = result + jnp.concatenate([low, high], axis=-1).astype(f32)
    return result.astype(bf16)


def solution(mesh):
    placed = (
        P(AXES, None),
        P(),
        P(),
        P(),
        P(),
        P(),
        P(),
        P(),
        P(),
        P(None, None, None, "width", None),
        P(),
    )

    shape = (FRAMES * mesh.shape["tm"], ROWS * mesh.shape["height"], COLS * mesh.shape["width"])
    sizes = (mesh.shape["tm"] // 2, 2, mesh.shape["height"], mesh.shape["width"])
    mesh = jax.sharding.Mesh(mesh.devices.reshape(sizes), AXES)
    return jax.shard_map(
        lambda *args: decode(*args, clip=shape),
        mesh=mesh,
        in_specs=placed,
        out_specs=P(TIME, "height", "width", None),
        check_vma=False,
    )
```

```python
import jax
import jax.numpy as jnp
from jax import lax
from jax.experimental import pallas as pl
from jax.experimental.pallas import tpu as pltpu
from jax.sharding import PartitionSpec as P


GROUPS = 32
FRAMES = 4
ROWS = 8
COLS = 8
AXES = ("ty", "tc", "height", "width")
TIME = ("ty", "tc")
bf16 = jnp.bfloat16
f32 = jnp.float32


def project_kernel(tok_ref, shift_ref, scale_ref, weight_ref, bias_ref, out_ref):
    values = tok_ref[...].astype(f32)
    center = jnp.mean(values, axis=-1, keepdims=True)
    values = values - center
    spread = jnp.mean(values * values, axis=-1, keepdims=True)
    normed = (values * lax.rsqrt(spread + 1e-06) * (1.0 + scale_ref[...]) + shift_ref[...]).astype(bf16)
    patches = lax.dot_general(normed, weight_ref[...], (((1,), (1,)), ((), ())), preferred_element_type=f32)
    patches = (patches + bias_ref[...]).astype(bf16)
    size = patches.shape[1]
    lat = size // 4
    source = lax.broadcasted_iota(jnp.int32, (size, size), 0)
    target = lax.broadcasted_iota(jnp.int32, (size, size), 1)
    wanted = 4 * (target % lat) + target // lat
    order = jnp.where(source == wanted, 1.0, 0.0).astype(bf16)
    patches = jnp.dot(patches, order, preferred_element_type=f32)
    half = patches.shape[0] // 2
    packed = jnp.concatenate([patches[:half], patches[half:]], axis=1).astype(bf16)
    out_ref[...] = jnp.broadcast_to(packed[None], out_ref.shape)


def project(tokens, shift_mod, scale_mod, proj_weight, proj_bias, copies):
    count, features = tokens.shape[0], proj_weight.shape[0]
    operands = (tokens, shift_mod[None], scale_mod[None], proj_weight, proj_bias[None])
    return pl.pallas_call(
        project_kernel,
        out_shape=pltpu.VMEM((copies, count // 2, 2 * features), bf16),
        compiler_params=pltpu.CompilerParams(vmem_limit_bytes=16 * 1024 * 1024),
        name="project",
    )(*[pltpu.with_memory_space_constraint(x, pltpu.HBM) for x in operands])


def prepare_kernel(w1_ref, b1_ref, gain_ref, nbias_ref, banded, affine):
    LAT, C = w1_ref.shape[3:]
    affine[0:1, :] = b1_ref[...]
    affine[1:2, :] = gain_ref[...]
    affine[2:3, :] = nbias_ref[...]

    for a in range(3):
        for v in range(2):
            for z in range(2):
                for i in range(2):
                    for j in range(2):
                        row = i if v == 0 else (-1 if i == 1 else 2)
                        col = j if z == 0 else (-1 if j == 1 else 2)
                        start = a * 16 * LAT + (((v * 2 + z) * 2 + i) * 2 + j) * LAT
                        for oi in range(2):
                            for oj in range(2):
                                b, e = row - oi + 1, col - oj + 1
                                at = (oi * 2 + oj) * C
                                if 0 <= b < 3 and 0 <= e < 3:
                                    banded[start : start + LAT, at : at + C] = w1_ref[a, b, e]
                                else:
                                    banded[start : start + LAT, at : at + C] = jnp.zeros((LAT, C), bf16)


def prepare(conv1_weight, conv1_bias, norm_gain, norm_bias):
    LAT, C = conv1_weight.shape[3:]
    vmem = pl.BlockSpec(memory_space=pltpu.VMEM)
    return pl.pallas_call(
        prepare_kernel,
        out_shape=(pltpu.VMEM((48 * LAT, 4 * C), bf16), pltpu.VMEM((3, C), f32)),
        in_specs=[vmem] * 4,
        out_specs=(vmem, vmem),
        compiler_params=pltpu.CompilerParams(vmem_limit_bytes=16 * 1024 * 1024),
        name="prepare",
    )(conv1_weight, conv1_bias[None], norm_gain[None], norm_bias[None])


def pair_products(blocks, w2_ref, TH):
    C, C2 = w2_ref.shape[3:]
    total = None
    for a in range(3):
        for b in range(3):
            taps = [block[b : b + TH].reshape(TH * block.shape[1], 3 * C) for block in blocks[a]]
            taps = jnp.concatenate(taps, axis=0)
            part = jnp.dot(taps, w2_ref[a, b].reshape(3 * C, C2), preferred_element_type=f32)
            total = part if total is None else total + part
    return total


def store_pairs(total, out):
    FT, TH, TW, C2 = out.shape
    total = total.reshape(FT // 2, TH, 2, TW, C2)
    for p in range(FT // 2):
        for k in range(2):
            out[2 * p + k] = total[p, :, k].astype(out.dtype)


def blocks_of(first, second, tile):
    return (
        [first.at[tile, 0], first.at[tile, 1], first.at[tile, 2]],
        [first.at[tile, 2], second.at[tile, 0], second.at[tile, 1]] if second is not None else None,
    )


def activate(t, pos_ref, hidden_early, hidden, norm, field, slot_of, TH):
    FT = FRAMES
    HP, WP = hidden.shape[1:3]
    C = norm.shape[1]
    R = TH + 2
    tm, height = pos_ref[0], pos_ref[1]
    gmean, slope, offset = norm[0:1, :], norm[1:2, :], norm[2:3, :]
    actual = tm * FT + t - 2
    frame = jnp.maximum(actual, 0)
    group, k = frame // FT, frame % FT
    mine = group % 2 == tm % 2
    early = mine & (k >= 2)
    slot_early = (group // 2) * (FT - 2) + jnp.maximum(k - 2, 0)
    slot = (group // 2) * (FT + 2) + jnp.where(mine, FT + jnp.minimum(k, 1), FT - 1 - k)
    for pp in range(TH // 2 + 2):
        prow = height * (TH // 2) - 1 + pp
        source = jnp.clip(prow, 0, HP - 1)
        inside = (actual >= 0) & (prow >= 0) & (prow < HP)
        for oi in range(2):
            row = 2 * pp + oi - 1
            if row < 0 or row >= R:
                continue
            for oj in range(2):
                at = (oi * 2 + oj) * C
                h = jnp.where(
                    early, hidden_early[slot_early, source, :, at : at + C], hidden[slot, source, :, at : at + C]
                )
                h = h.astype(bf16).astype(f32)
                half = (h - gmean) * slope + offset
                act = half * jnp.tanh(half) + half
                act = jnp.where(inside, act, 0.0)
                for plane in range(field.shape[0]):
                    part = act[:, plane * 128 : (plane + 1) * 128]
                    if C < 128:
                        part = jnp.concatenate([part, jnp.zeros((WP, 128 - C), f32)], axis=1)
                    field[plane, slot_of(t) * R + row, pl.ds(8 + oj, WP, stride=2), :] = part


def clear_edges(field, W):
    edge = jnp.zeros(field.shape[:2] + (1, 128), f32)
    field[:, :, 7:8, :] = edge
    field[:, :, 8 + W : 9 + W, :] = edge


def columns(sources, cols, k, TW):
    tiles, _, R = cols.shape[:3]
    C = cols.shape[4] // 3
    for r in range(R):
        for tile in range(tiles):
            for e in range(3):
                at = 7 + e + tile * TW
                for plane in range(sources[0][0].shape[0]):
                    lanes = min(C, 128)
                    lane_at = e * C + plane * 128
                    parts = [field[plane, slot * R + r, at : at + TW, :] for field, slot in sources]
                    part = jnp.concatenate(parts, axis=0).astype(bf16)
                    cols[tile, k, r, :, lane_at : lane_at + lanes] = part[:, :lanes]


def send_pair(which, first, second, w2_ref, width, other_ref, TH):
    steps = other_ref.shape[0]
    for step in range(steps):
        tile = lax.rem(width + step + 1, steps + 1)
        total = pair_products([[block] for block in blocks_of(first, second, tile)[which]], w2_ref, TH)
        store_pairs(total, other_ref.at[step])


def send_kernel(pos_ref, hidden_early, hidden, norm, field_first, first, w2_ref, other_ref, second, field):
    TH, TW = other_ref.shape[2:4]
    FT = FRAMES
    clear_edges(field, first.shape[0] * TW)
    for t in range(FT, FT + 2):
        activate(t, pos_ref, hidden_early, hidden, norm, field, lambda t: t - FT, TH)
    columns([(field_first, FT - 1), (field, 0)], second, 0, TW)
    columns([(field, 0), (field, 1)], second, 1, TW)

    def once(k, carry):
        send_pair(1, first, second, w2_ref, pos_ref[2] + k, other_ref, TH)
        return carry

    once(0, 0)


def own_kernel(pos_ref, first, second, w2_ref, own_ref):
    low, high = blocks_of(first, second, pos_ref[2])
    total = pair_products([[x, y] for x, y in zip(low, high)], w2_ref, own_ref.shape[1])
    store_pairs(total, own_ref)


def window_writer(rows, HP, WP, LAT):
    frame_rows = HP * WP
    LN = 8 * LAT
    lane = lax.broadcasted_iota(jnp.int32, (rows, LN), 1)
    q = lax.broadcasted_iota(jnp.int32, (rows, LN), 0) % WP
    j_one = (lane // LAT) % 2 == 1
    low = lane < LN // 2
    keep = (j_one & (q > 0)) | (jnp.logical_not(j_one) & (q < WP - 1))
    i_one = (lax.broadcasted_iota(jnp.int32, (frame_rows, LN), 1) // (2 * LAT)) % 2 == 1

    def write(window, slot, latent_ref, first):
        pieces = []
        for k in range(frame_rows // (2 * rows)):
            x = latent_ref[first + k].astype(f32)
            z = jnp.where(j_one, pltpu.roll(x, 1, 0), pltpu.roll(x, rows - 1, 0))
            z = jnp.where(keep, z, 0.0)
            zr = pltpu.roll(z, LN // 2, 1)
            xr = pltpu.roll(x, LN // 2, 1)
            pieces.append(jnp.where(low, x, zr))
            pieces.append(jnp.where(low, xr, z))
        y = jnp.concatenate(pieces, axis=0)
        zero = jnp.zeros((WP, LN), f32)
        above = jnp.concatenate([zero, y[:-WP]], axis=0)
        below = jnp.concatenate([y[WP:], zero], axis=0)
        v = jnp.where(i_one, above, below)
        window[slot, :, 0:LN] = y.astype(bf16)
        window[slot, :, LN : 2 * LN] = v.astype(bf16)

    return write


def hidden_frames(frames, banded, bias, out, first, sums):
    C = bias.shape[1]
    s, sq = sums
    for n in range(4):
        taps = jnp.concatenate(
            [jnp.concatenate([frame[a]() for frame in frames], axis=0) for a in range(3)], axis=1
        )
        h = jnp.dot(taps, banded[:, n * C : (n + 1) * C], preferred_element_type=f32) + bias
        out[first : first + len(frames), :, :, n * C : (n + 1) * C] = h.reshape((len(frames),) + out.shape[1:3] + (C,))
        h8 = h.reshape(h.shape[0] // 8, 8, C)
        s = s + jnp.sum(h8, axis=0)
        sq = sq + jnp.sum(h8 * h8, axis=0)
    return s, sq


def loader(window, slot):
    return lambda: window[slot]


def early_kernel(mine_ref, banded, affine, window, hidden, sums, *, HP, WP, FT):
    TY = (window.shape[0] - 2) // FT
    chunks = mine_ref.shape[0] // (TY * FT)
    C = affine.shape[1]
    write = window_writer(mine_ref.shape[1], HP, WP, banded.shape[0] // 48)
    window[TY * FT :] = jnp.zeros((2,) + window.shape[1:], bf16)
    totals = (jnp.zeros((8, C), f32), jnp.zeros((8, C), f32))
    for ty in range(TY):
        for k in range(FT):
            write(window, ty * FT + k, mine_ref, (ty * FT + k) * chunks)
    for ty in range(TY):
        frames = [[loader(window, ty * FT + k + a - 2) for a in range(3)] for k in range(2, FT)]
        totals = hidden_frames(frames, banded, affine[0:1, :], hidden, ty * (FT - 2), totals)
    sums[0:8, :] = totals[0]
    sums[8:16, :] = totals[1]


def decode_kernel(
    pos_ref,
    theirs_ref,
    window_mine,
    hidden_early,
    sums_early,
    banded,
    affine,
    w2_hbm,
    other_ref,
    cols,
    w2_ref,
    hidden,
    norm,
    field,
    window,
    sem,
    *,
    NT,
    HP,
    WP,
    FT,
    TH,
    TW,
):
    C = w2_ref.shape[3]
    W = 2 * WP
    tm, width = pos_ref[0], pos_ref[2]
    tc = tm % 2
    copy = pltpu.make_async_copy(w2_hbm, w2_ref, sem)
    copy.start()

    TY = NT // (2 * FT)
    chunks = theirs_ref.shape[0] // (TY * FT)
    write = window_writer(theirs_ref.shape[1], HP, WP, banded.shape[0] // 48)
    window[TY * FT :] = jnp.zeros((2,) + window.shape[1:], bf16)
    for ty in range(TY):
        for k in range(FT):
            write(window, ty * FT + k, theirs_ref, (ty * FT + k) * chunks)

    s, sq = sums_early[0:8, :], sums_early[8:16, :]
    for ty in range(TY):
        same = ty * FT + FT - 2
        previous = (ty - 1) * FT + FT - 2 if ty > 0 else TY * FT
        before_mine = jnp.where(tc == 1, same, previous)
        before_theirs = jnp.where(tc == 1, previous, same)
        sequence_mine = [loader(window, before_mine + k) for k in range(2)]
        sequence_mine += [loader(window_mine, ty * FT + k) for k in range(2)]
        sequence_theirs = [loader(window_mine, before_theirs + k) for k in range(2)]
        sequence_theirs += [loader(window, ty * FT + k) for k in range(FT)]
        frames = [sequence_theirs[k : k + 3] for k in reversed(range(FT))] + [sequence_mine[k : k + 3] for k in range(2)]
        s, sq = hidden_frames(frames, banded, affine[0:1, :], hidden, ty * (FT + 2), (s, sq))
    s = jnp.broadcast_to(jnp.sum(s, axis=0, keepdims=True), (8, C))
    sq = jnp.broadcast_to(jnp.sum(sq, axis=0, keepdims=True), (8, C))
    size = C * lax.axis_size("width") // GROUPS
    member = jnp.where(
        lax.broadcasted_iota(jnp.int32, (C, C), 0) // size == lax.broadcasted_iota(jnp.int32, (C, C), 1) // size, 1.0, 0.0
    )
    count = NT * HP * WP * 4 * size
    gmean = jnp.dot(s, member, preferred_element_type=f32, precision=lax.Precision.HIGHEST)[0:1] / count
    second = jnp.dot(sq, member, preferred_element_type=f32, precision=lax.Precision.HIGHEST)[0:1] / count
    gvar = second - gmean * gmean
    inverse = lax.rsqrt(gvar + 1e-06)
    norm[0:1, :] = gmean
    norm[1:2, :] = 0.5 * inverse * affine[1:2, :]
    norm[2:3, :] = 0.5 * affine[2:3, :]

    clear_edges(field, W)

    def act_body(t, carry):
        activate(t, pos_ref, hidden_early, hidden, norm, field, lambda t: t, TH)
        return carry

    lax.fori_loop(0, FT, act_body, 0, unroll=2)

    def pair_body(t, carry):
        columns([(field, t), (field, t + 1)], cols, t, TW)
        return carry

    lax.fori_loop(0, FT - 1, pair_body, 0, unroll=3)
    copy.wait()

    def once(k, carry):
        send_pair(0, cols, None, w2_ref, width + k, other_ref, TH)
        return carry

    once(0, 0)


def decode(
    tokens,
    shift_mod,
    scale_mod,
    proj_weight,
    proj_bias,
    conv1_weight,
    conv1_bias,
    norm_gain,
    norm_bias,
    conv2_weight,
    conv2_bias,
    *,
    clip,
):
    width_count = lax.axis_size("width")
    height_count = lax.axis_size("height")
    time_count = lax.axis_size(TIME)
    devices = width_count * height_count * time_count
    NT, NH, NW = clip
    FT, TH, TW = FRAMES, ROWS, COLS
    C2 = conv2_weight.shape[4]
    HP, WP = NH // 2, NW // 2
    C = conv2_weight.shape[3]
    LAT = conv1_weight.shape[3]

    spread = project(tokens, shift_mod, scale_mod, proj_weight, proj_bias, devices // 2)
    mine = lax.all_to_all(spread, ("ty", "height", "width"), 0, 0, tiled=True)
    theirs = lax.ppermute(mine, "tc", [(0, 1), (1, 0)])

    width = lax.axis_index("width")
    position = jnp.stack([lax.axis_index(TIME), lax.axis_index("height"), width]).astype(jnp.int32)
    take = lambda x, axis: lax.dynamic_slice_in_dim(x, width * C, C, axis)
    smem = pl.BlockSpec(memory_space=pltpu.SMEM)
    vmem = pl.BlockSpec(memory_space=pltpu.VMEM)
    resident = lambda x: pltpu.with_memory_space_constraint(x, pltpu.VMEM)
    conv2_weight = pltpu.with_memory_space_constraint(conv2_weight, pltpu.HBM)
    mine, theirs = resident(mine), resident(theirs)
    banded, affine = prepare(
        take(conv1_weight, 4), take(conv1_bias, 0), take(norm_gain, 0), take(norm_bias, 0)
    )
    banded, affine = resident(banded), resident(affine)
    TY = time_count // 2
    window, hidden, sums = pl.pallas_call(
        lambda *refs: early_kernel(*refs, HP=HP, WP=WP, FT=FT),
        out_shape=(
            pltpu.VMEM((TY * FT + 2, HP * WP, 16 * LAT), bf16),
            pltpu.VMEM((TY * (FT - 2), HP, WP, 4 * C), f32),
            pltpu.VMEM((16, C), f32),
        ),
        in_specs=[vmem, vmem, vmem],
        out_specs=(vmem, vmem, vmem),
        compiler_params=pltpu.CompilerParams(vmem_limit_bytes=12 * 1024 * 1024),
        name="early",
    )(mine, banded, affine)
    window, hidden, sums = resident(window), resident(hidden), resident(sums)
    sent = pltpu.VMEM((width_count - 1, FT // 2, TH, TW, C2), bf16)
    columns_of = lambda pairs: pltpu.VMEM((width_count, pairs, TH + 2, 2 * TW, 3 * C), bf16)
    field_of = lambda frames: pltpu.VMEM((pl.cdiv(C, 128), frames * (TH + 2), NW + 16, 128), f32)
    other, first, w2, rest, norm, field = pl.pallas_call(
        lambda *refs: decode_kernel(*refs, NT=NT, HP=HP, WP=WP, FT=FT, TH=TH, TW=TW),
        out_shape=(
            sent,
            columns_of(FT - 1),
            pltpu.VMEM(conv2_weight.shape, bf16),
            pltpu.VMEM((TY * (FT + 2), HP, WP, 4 * C), f32),
            pltpu.VMEM((3, C), f32),
            field_of(FT),
        ),
        in_specs=[smem] + [vmem] * 6 + [pl.BlockSpec(memory_space=pl.ANY)],
        out_specs=(vmem,) * 6,
        scratch_shapes=[
            pltpu.VMEM((TY * FT + 2, HP * WP, 16 * LAT), bf16),
            pltpu.SemaphoreType.DMA,
        ],
        compiler_params=pltpu.CompilerParams(vmem_limit_bytes=14 * 1024 * 1024),
        name="decode",
    )(position, theirs, window, hidden, sums, banded, affine, conv2_weight)
    first, w2, rest, norm, field = [resident(x) for x in (first, w2, rest, norm, field)]

    def exchange(other):
        return [
            lax.ppermute(other[step - 1], "width", [(k, (k + step) % width_count) for k in range(width_count)])
            for step in range(1, width_count)
        ]

    moved_low = exchange(other)
    other, second = pl.pallas_call(
        send_kernel,
        out_shape=(sent, columns_of(2)),
        in_specs=[smem] + [vmem] * 6,
        out_specs=(vmem, vmem),
        scratch_shapes=[field_of(2)],
        compiler_params=pltpu.CompilerParams(vmem_limit_bytes=8 * 1024 * 1024),
        name="send",
    )(position, hidden, rest, norm, field, first, w2)
    moved_high = exchange(other)
    result = pl.pallas_call(
        own_kernel,
        out_shape=pltpu.VMEM((FT, TH, TW, C2), f32),
        in_specs=[smem, vmem, vmem, vmem],
        out_specs=vmem,
        compiler_params=pltpu.CompilerParams(vmem_limit_bytes=8 * 1024 * 1024),
        name="own",
    )(position, first, resident(second), w2)
    result = result + conv2_bias
    for low, high in zip(moved_low, moved_high):
        result = result + jnp.concatenate([low, high], axis=0).astype(f32)
    return result.astype(bf16)


def solution(mesh):
    placed = (
        P(AXES, None),
        P(),
        P(),
        P(),
        P(),
        P(),
        P(),
        P(),
        P(),
        P(None, None, None, "width", None),
        P(),
    )

    shape = (FRAMES * mesh.shape["tm"], ROWS * mesh.shape["height"], COLS * mesh.shape["width"])
    sizes = (mesh.shape["tm"] // 2, 2, mesh.shape["height"], mesh.shape["width"])
    mesh = jax.sharding.Mesh(mesh.devices.reshape(sizes), AXES)
    return jax.shard_map(
        lambda *args: decode(*args, clip=shape),
        mesh=mesh,
        in_specs=placed,
        out_specs=P(TIME, "height", "width", None),
        check_vma=False,
    )
```
